32 devices in a mesh: tm: 8 (over z, y), tensor: 4 (over x, core).
Axes of the slice: x: 2, y: 2, z: 4, core: 2. Of those that a mesh axis runs over, the one named last changes fastest.
Arguments:
- frames_in: bfloat16 [8, 1024, 768], P('tm'), may hold values from -16 to 16
- norm_gain: float32 [768], replicated, may hold values from 0.1 to 1.9
- w_qkv: bfloat16 [768, 3, 768], P(None, None, 'tensor'), may hold values from -0.21650635 to 0.21650635
- w_out: bfloat16 [768, 768], P('tensor'), may hold values from -0.21875 to 0.21875
- keep_runs: int32 [8, 16, 2], replicated, may hold values from 0 to 1023, as said below
- out_cotangent: bfloat16 [8, 1024, 768], P('tm'), may hold values from -6 to 6
Outputs:
- block_out: bfloat16 [8, 1024, 768], P('tm', None, 'tensor')
- grad_in: bfloat16 [8, 1024, 768], P('tm', None, 'tensor')
- grad_qkv: bfloat16 [768, 3, 768], P('tm', None, 'tensor')
- grad_proj: bfloat16 [768, 768], P('tensor', 'tm')
- grad_gain: float32 [768], P('tensor')
The draws below stay inside these ranges and needn't reach their ends.
Inputs may be any that keep to these rules, and one draw needn't show every extreme that they name: keep_runs[t, r] = (first, length) is the r-th run of kept positions of frame t; the 16 runs of a frame are disjoint, in rising order, and lie within the frame's 1024 positions.
All inputs are finite; a program needn't handle non-finite values.
Results may differ from the reference program's by a relative error of at most 0.034.
Values may be sent and summed in bfloat16 or wider, within the bound.
No kernel may reach another device: no remote copies, remote signals or barrier semaphores. Data moves between devices by JAX's collectives and lax.ppermute only.
A program may use at most 128 MiB of HBM per device.

```python
import jax
import jax.numpy as jnp
from jax import lax

D = 768
H = 12
P_SIZE = 1024
F_DEV = 1
R = 16
F = 8


def draw_keep_runs(key, part):
    run_block = P_SIZE // R
    length_key, offset_key = jax.random.split(jax.random.fold_in(key, 7))
    lengths = jax.random.randint(length_key, (F, R), 1, 4 * run_block // 5 + 1)
    offsets = jax.random.randint(offset_key, (F, R), 0, run_block - lengths + 1)
    starts = jnp.arange(R, dtype=jnp.int32)[None, :] * run_block + offsets
    return jnp.stack([starts, lengths], axis=-1).astype(jnp.int32)


def draw_frames_in(key, part):
    keys = jax.random.split(jax.random.fold_in(key, 11), 2)
    groups = F // F_DEV
    block_width = D // groups
    drawn = jax.random.normal(keys[0], (F, P_SIZE, D), jnp.float32)
    chosen = jax.random.permutation(keys[1], groups)
    frame_block = chosen[jnp.arange(F) // F_DEV]
    feature_block = jnp.arange(D) // block_width
    boost = jnp.where(feature_block[None, :] == frame_block[:, None], 3.0, 1.0)
    tokens = drawn * boost[:, None, :]
    return jnp.clip(tokens, -16.0, 16.0).astype(jnp.bfloat16)


def draw_w_qkv(key, part):
    base_key = jax.random.fold_in(jax.random.fold_in(key, 23), 0)
    limit = 6.0 * D ** (-0.5)
    base = jax.random.normal(base_key, (D, 3, D), jnp.float32) * D ** (-0.5)
    return jnp.clip(base, -limit, limit).astype(jnp.bfloat16)


def strengthened(drawn, key, source, target, blocks, factor):
    def block_of(axis_at):
        return (jnp.arange(drawn.shape[axis_at]) // (drawn.shape[axis_at] // blocks)).reshape((-1,) + (1,) * (drawn.ndim - 1 - axis_at))

    one_side = jax.random.permutation(key, blocks)[block_of(target)]
    far = (block_of(target) + blocks // 2) % blocks
    return jnp.where((block_of(source) == one_side) | (block_of(source) == far), factor * drawn, drawn)


def block_levels(stream_key, shape, cuts, smallest, largest):
    loudness = 1.0
    for dim, parts in cuts:
        draws = jax.random.uniform(jax.random.fold_in(jax.random.fold_in(stream_key, 6), dim), (parts,), jnp.float32, smallest / len(cuts), largest / len(cuts))
        loudness = loudness * jnp.repeat(jnp.exp(draws), shape[dim] // parts).reshape((-1,) + (1,) * (len(shape) - 1 - dim))
    return loudness


def centred(key, dims, deviation, most, cuts=(), kind=jnp.bfloat16):
    gain = block_levels(key, dims, cuts, -0.22, 0.18) if cuts else 1.0
    drawn = jax.random.normal(key, dims, jnp.float32) * deviation * gain
    return jnp.minimum(jnp.maximum(drawn, -most), most).astype(kind)


def noise_with(key, extent, width, most, shards, heavy, kind=jnp.bfloat16):
    drawn = width * jax.random.normal(key, extent, jnp.float32)
    if shards:
        drawn = drawn * block_levels(key, extent, shards, -0.22, 0.18)
    return jnp.clip(strengthened(drawn, jax.random.fold_in(key, 3), *heavy), -most, most).astype(kind)


def setup_inputs(seed: int = 0) -> dict:
    splits = jax.random.split(jax.random.key(seed), 7)
    return {
        "frames_in": draw_frames_in(jax.random.fold_in(splits[6], 71), 0),
        "norm_gain": jnp.clip(1.0 + 0.18 * jax.random.normal(splits[1], (D,), jnp.float32), 0.1, 1.9),
        "w_qkv": draw_w_qkv(jax.random.fold_in(splits[6], 71), 0),
        "w_out": centred(splits[3], (D, D), D ** -0.5, 0.21875, ((0, 4),)),
        "keep_runs": draw_keep_runs(jax.random.fold_in(splits[6], 71), 0),
        "out_cotangent": noise_with(splits[5], (F, P_SIZE, D), 1.0, 6.0, ((0, 8),), (0, 2, 8, 2.0)),
    }


epsilon = 1e-05

def kept_table(keep_runs, first_place, place_count):
    places = first_place + jnp.arange(place_count, dtype=jnp.int32)
    starts = keep_runs[:, :, 0:1]
    lengths = keep_runs[:, :, 1:2]
    inside = (places[None, None, :] >= starts) & (places[None, None, :] < starts + lengths)
    return lax.optimization_barrier(jnp.sum(inside.astype(jnp.int32), axis=1)).astype(jnp.int32)

def normalize(frames_in):
    frames_float = frames_in.astype(jnp.float32)
    centre = lax.optimization_barrier(jnp.mean(frames_float, axis=-1, keepdims=True))
    shifted = frames_float - centre
    spread = lax.optimization_barrier(jnp.mean(shifted * shifted, axis=-1, keepdims=True))
    inverse_spread = lax.rsqrt(spread + epsilon)
    return (frames_float, shifted * inverse_spread, inverse_spread)

def attend(packed, kept_mask):
    frames, places, row_width = packed.shape
    head_width = D // H
    pieces = packed.reshape(frames, places, 3, row_width // (3 * head_width), head_width)
    scores = jnp.einsum('tphd,uphd->phtu', pieces[:, :, 0].astype(jnp.float32), pieces[:, :, 1].astype(jnp.float32))
    scores = scores * head_width ** (-0.5)
    allowed = jnp.transpose(kept_mask)[:, None, None, :] > 0
    scores = jnp.where(allowed, scores, -1000000000.0)
    row_max = lax.optimization_barrier(jnp.max(scores, axis=-1, keepdims=True))
    exponent = jnp.exp(scores - row_max)
    weights = (exponent / lax.optimization_barrier(jnp.sum(exponent, axis=-1, keepdims=True))).astype(jnp.bfloat16)
    mixed_rows = jnp.einsum('phtu,uphd->tphd', weights.astype(jnp.float32), pieces[:, :, 2].astype(jnp.float32))
    mixed_rows = jnp.where(kept_mask[:, :, None, None] > 0, mixed_rows, 0.0)
    return mixed_rows.astype(jnp.bfloat16).reshape(frames, places, row_width // 3)

def forward(frames_in, norm_gain, w_qkv, w_out, kept_mask):
    frames_float, standard, inverse_spread = normalize(frames_in)
    normed = (standard * norm_gain).astype(jnp.bfloat16)
    packed = jnp.dot(normed.reshape(F * P_SIZE, D), w_qkv.reshape(D, 3 * D), preferred_element_type=jnp.float32)
    packed = packed.astype(jnp.bfloat16).reshape(F, P_SIZE, 3 * D)
    mixed_rows = attend(packed, kept_mask)
    branch = jnp.dot(mixed_rows.reshape(F * P_SIZE, D), w_out, preferred_element_type=jnp.float32).reshape(F, P_SIZE, D)
    return (frames_float + branch).astype(jnp.bfloat16)

def reference(frames_in, norm_gain, w_qkv, w_out, keep_runs, out_cotangent):
    kept_mask = kept_table(keep_runs, 0, P_SIZE)

    def apply_block(first_arg, second_arg, third_arg, fourth_arg):
        return forward(first_arg, second_arg, third_arg, fourth_arg, kept_mask)
    block_out, pullback = jax.vjp(apply_block, frames_in, norm_gain, w_qkv, w_out)
    grad_in, grad_gain, grad_qkv, grad_proj = pullback(out_cotangent)
    return (block_out, grad_in, grad_qkv, grad_proj, grad_gain)
```

```python
import functools

import jax
import jax.numpy as jnp
from jax import lax
from jax.experimental import pallas as pl
from jax.experimental.pallas import tpu as pltpu
from jax.sharding import PartitionSpec as P

D = 768
H = 12
HEAD = D // H
LANES = 128
EPS = 1e-05
MASKED = -1000000000.0

BF = jnp.bfloat16
F32 = jnp.float32


def exchange(value, axis, bit):
    size = lax.axis_size(axis)
    return lax.ppermute(value, axis, [(i, i ^ bit) for i in range(size)])


def dot(a, b):
    return lax.dot_general(a, b, (((1,), (0,)), ((), ())), preferred_element_type=F32)


def dot_t(a, b):
    return lax.dot_general(a, b, (((1,), (1,)), ((), ())), preferred_element_type=F32)


def t_dot(a, b):
    return lax.dot_general(a, b, (((0,), (0,)), ((), ())), preferred_element_type=F32)


def standardize(x):
    x = x.astype(F32)
    shifted = x - jnp.mean(x, axis=-1, keepdims=True)
    inverse = lax.rsqrt(jnp.mean(shifted * shifted, axis=-1, keepdims=True) + EPS)
    return shifted * inverse, inverse


def block_rows(value, frames, b, rows):
    q = value.shape[0] // frames
    if q == rows:
        return value
    cut = value.reshape(frames, q, value.shape[1])[:, b * rows : (b + 1) * rows]
    return cut.reshape(frames * rows, value.shape[1])


def put_rows(ref, g, b, rows, col, value):
    frames = ref.shape[1]
    ref[g, :, b * rows : (b + 1) * rows, col : col + value.shape[1]] = value.reshape(
        frames, rows, value.shape[1]
    )


def split_heads(value):
    lane = lax.broadcasted_iota(jnp.int32, value.shape, 1)
    zero = jnp.zeros_like(value)
    return jnp.concatenate(
        [jnp.where(lane < HEAD, value, zero), jnp.where(lane >= HEAD, value, zero)], axis=0
    )


def join_heads(value):
    n = value.shape[0] // 2
    lane = lax.broadcasted_iota(jnp.int32, (n, value.shape[1]), 1)
    return jnp.where(lane < HEAD, value[:n], value[n:])


def forward_kernel(
    frames, rows, who, xo, xp, gain, wcat, wout, mask, normed, packed, weights, mixed, keep, send
):
    hi = who[0] // 2
    width = wout.shape[0]
    half = wout.shape[1] // 2
    tokens = xo.shape[0]
    for g, x in enumerate((xo, xp)):
        standard, _ = standardize(x[...])
        n = (standard * gain[...]).astype(BF)
        normed[g] = n
        pk = dot(n, wcat[...]).astype(BF)
        packed[g] = pk
        for b in range(tokens // (frames * rows)):
            inside = mask[g, b]
            for p in range(width // LANES):
                q = block_rows(pk[:, p * LANES : (p + 1) * LANES], frames, b, rows)
                k = block_rows(pk[:, width + p * LANES : width + (p + 1) * LANES], frames, b, rows)
                v = block_rows(
                    pk[:, 2 * width + p * LANES : 2 * width + (p + 1) * LANES], frames, b, rows
                )
                s = dot_t(q, split_heads(k)) * HEAD ** (-0.5)
                n_rows = frames * rows
                both = []
                for e in range(2):
                    part = jnp.where(inside > 0, s[:, e * n_rows : (e + 1) * n_rows], MASKED)
                    top = jnp.max(part, axis=-1, keepdims=True)
                    ex = jnp.exp(part - top) * inside
                    total = jnp.sum(ex, axis=-1, keepdims=True)
                    total = jnp.where(total > 0, total, 1.0)
                    both.append((ex / total).astype(BF))
                w = jnp.concatenate(both, axis=1)
                weights[g, b, p] = w
                put_rows(mixed, g, b, rows, p * LANES, dot(w, split_heads(v)).astype(BF))
        m = mixed[g].reshape(tokens, width)
        y = dot(m, wout[...])
        low, high = y[:, :half], y[:, half:]
        keep[g] = jnp.where(hi == 0, low, high)
        send[g] = jnp.where(hi == 0, high, low).astype(BF)


def backward_kernel(
    frames, rows, who, co, cp, packed, weights, normed, gain, wcat, wout, pcot, keep, send, stats,
    gains
):
    hi = who[0] // 2
    width = wout.shape[0]
    half = wout.shape[1] // 2
    tokens = co.shape[0]
    total_gain = jnp.zeros((1, wout.shape[1]), F32)
    for g, c in enumerate((co, cp)):
        mc = dot_t(c[...], wout[...]).astype(BF)
        pk = packed[g]
        for b in range(tokens // (frames * rows)):
            for p in range(width // LANES):
                q = block_rows(pk[:, p * LANES : (p + 1) * LANES], frames, b, rows)
                k = block_rows(pk[:, width + p * LANES : width + (p + 1) * LANES], frames, b, rows)
                v = block_rows(
                    pk[:, 2 * width + p * LANES : 2 * width + (p + 1) * LANES], frames, b, rows
                )
                dm = block_rows(mc[:, p * LANES : (p + 1) * LANES], frames, b, rows)
                dw = dot_t(dm, split_heads(v)).astype(BF).astype(F32)
                w = weights[g, b, p]
                n_rows = frames * rows
                both = []
                for e in range(2):
                    we = w[:, e * n_rows : (e + 1) * n_rows].astype(F32)
                    de = dw[:, e * n_rows : (e + 1) * n_rows]
                    inner = jnp.sum(we * de, axis=-1, keepdims=True)
                    both.append((we * (de - inner) * HEAD ** (-0.5)).astype(BF))
                ds = jnp.concatenate(both, axis=1)
                dq = dot(ds, split_heads(k)).astype(BF)
                dk = join_heads(t_dot(ds, q)).astype(BF)
                dv = join_heads(t_dot(w, dm)).astype(BF)
                put_rows(pcot, g, b, rows, p * LANES, dq)
                put_rows(pcot, g, b, rows, width + p * LANES, dk)
                put_rows(pcot, g, b, rows, 2 * width + p * LANES, dv)
        pc = pcot[g].reshape(tokens, 3 * width)
        nc = dot_t(pc, wcat[...])
        nn = normed[g].astype(F32) * nc
        mean_plain = jnp.sum(nc * gain[...], axis=-1, keepdims=True)
        mean_cross = jnp.sum(nn, axis=-1, keepdims=True)
        total_gain = total_gain + jnp.sum(nn, axis=0, keepdims=True)
        lane = lax.broadcasted_iota(jnp.int32, (tokens, LANES), 1)
        both = jnp.where(lane == 0, mean_plain, mean_cross) * (1.0 / wout.shape[1])
        stats[:, g * tokens : (g + 1) * tokens] = both.T[:8]
        low, high = nc[:, :half], nc[:, half:]
        keep[g] = jnp.where(hi == 0, low, high)
        send[g] = jnp.where(hi == 0, high, low).astype(BF)
    gains[...] = total_gain / gain[...]


def grads_kernel(normed, pcot, co, cp, mixed, keep, send):
    width = mixed.shape[2]
    share = width // 2
    n = [normed[0], normed[1]]
    c = [co[...], cp[...]]
    columns = []
    for which in range(3):
        cols = slice(which * width, (which + 1) * width)
        columns.append(t_dot(n[0], pcot[0][:, cols]) + t_dot(n[1], pcot[1][:, cols]))
    columns.append(t_dot(c[0], mixed[0]) + t_dot(c[1], mixed[1]))
    keep[...] = jnp.concatenate([v[:, :share] for v in columns], axis=1)
    send[...] = jnp.concatenate([v[:, share:] for v in columns], axis=1).astype(BF)


def halves(value, who):
    half = value.shape[-1] // 2
    return jnp.where(who[0] // 2 == 0, value[..., :half], value[..., half:])


def own_and_other(value, who):
    share = value.shape[-1] // 2
    low, high = value[..., :share], value[..., share:]
    first = who[0] % 2 == 0
    return jnp.where(first, low, high), jnp.where(first, high, low)


def finish_forward_kernel(who, xo, xp, keep, recv, own, swap):
    for g, x in enumerate((xo, xp)):
        out = halves(x[...].astype(F32), who) + keep[g] + recv[1 - g].astype(F32)
        a, b = own_and_other(out, who)
        own[g] = a.astype(BF)
        swap[g] = b.astype(BF)


def finish_backward_kernel(who, xo, xp, co, cp, gain, keep, recv, stats, stats_in, own, swap):
    tokens = xo.shape[0]
    for g, (x, c) in enumerate(((xo, co), (xp, cp))):
        standard, inverse = standardize(x[...])
        both = (
            stats[:, g * tokens : (g + 1) * tokens]
            + stats_in[:, (1 - g) * tokens : (2 - g) * tokens]
        ).T
        mean_plain, mean_cross = both[:, 0:1], both[:, 1:2]
        scaled = (keep[g] + recv[1 - g].astype(F32)) * halves(gain[...], who)
        through = inverse * (scaled - mean_plain - halves(standard, who) * mean_cross)
        out = halves(c[...].astype(F32), who) + through
        a, b = own_and_other(out, who)
        own[g] = a.astype(BF)
        swap[g] = b.astype(BF)


def pack_kernel(own, recv, out):
    for g in range(2):
        out[:, g] = jnp.concatenate([own[g], recv[g]], axis=-1)


def assemble_kernel(who, first, second, out_first, out_second):
    share = out_first.shape[-1]
    j = who[0]
    for src, dst in ((first, out_first), (second, out_second)):
        for g in range(2):
            v = src[:, g]
            dst[:, j ^ (2 * g)] = v[:, :, :share]
            dst[:, j ^ (2 * g + 1)] = v[:, :, share:]


def call(kernel, outs, *args, scalars=1, name=None):
    specs = [pl.BlockSpec(memory_space=pltpu.SMEM)] * scalars + [
        pl.BlockSpec(memory_space=pltpu.VMEM)
    ] * (len(args) - scalars)
    shapes = [jax.ShapeDtypeStruct(shape, kind) for shape, kind in outs]
    return pl.pallas_call(
        kernel,
        out_shape=shapes,
        in_specs=specs,
        out_specs=[pl.BlockSpec(memory_space=pltpu.VMEM)] * len(outs),
        name=name,
        compiler_params=pltpu.CompilerParams(vmem_limit_bytes=56 * 1024 * 1024),
    )(*args)


def body(frames_in, norm_gain, w_qkv, w_out, keep_runs, out_cotangent):
    _, place_total, width = frames_in.shape
    n_tm, n_te = lax.axis_size("tm"), lax.axis_size("tensor")
    frames = n_tm
    chunk = place_total // (n_tm * n_te)
    tokens = frames * chunk
    rows = min(16, chunk)
    if (chunk % rows) or rows < 16:
        rows = chunk
    k = lax.axis_index("tm")
    j = lax.axis_index("tensor")
    who = j.astype(jnp.int32).reshape(1)
    share = w_qkv.shape[2]
    pair = 2 * share
    half = width // 2

    def gather_positions(value):
        mine = lax.dynamic_index_in_dim(
            value.reshape(n_tm, n_te, chunk, width), j, 1, keepdims=False
        )
        return lax.all_to_all(mine, "tm", split_axis=0, concat_axis=0, tiled=True)

    xo3 = gather_positions(frames_in)
    co3 = gather_positions(out_cotangent)
    xp = exchange(xo3, "tensor", 2).reshape(tokens, width)
    cp = exchange(co3, "tensor", 2).reshape(tokens, width)
    xo, co = xo3.reshape(tokens, width), co3.reshape(tokens, width)

    w_flat = w_qkv.reshape(width, 3 * share)
    w_other = exchange(w_flat, "tensor", 1)
    wcat = jnp.concatenate(
        [
            part[:, which * share : (which + 1) * share]
            for which in range(3)
            for part in (w_flat, w_other)
        ],
        axis=1,
    )
    wout = jnp.concatenate([w_out, exchange(w_out, "tensor", 1)], axis=0)
    gain = norm_gain.reshape(1, width)

    starts = keep_runs[:, :, 0]
    ends = starts + keep_runs[:, :, 1]
    chunks = jnp.stack([j, j ^ 2])
    places = (
        k * (n_te * chunk) + chunks[:, None] * chunk + jnp.arange(chunk, dtype=jnp.int32)[None, :]
    )
    kept = jnp.any(
        (places[:, None, None, :] >= starts[None, :, :, None])
        & (places[:, None, None, :] < ends[None, :, :, None]),
        axis=2,
    )
    kept = kept.reshape(2, frames, chunk // rows, rows).transpose(0, 2, 1, 3)
    kept = kept.reshape(2, chunk // rows, frames * rows)
    place_of = jnp.arange(frames * rows, dtype=jnp.int32) % rows
    mask = (
        kept[:, :, :, None] & kept[:, :, None, :] & (place_of[:, None] == place_of[None, :])
    ).astype(F32)

    n_blocks = chunk // rows
    n_rows = frames * rows
    normed, packed, weights, mixed4, keep_f, send_f = call(
        functools.partial(forward_kernel, frames, rows),
        [
            ((2, tokens, width), BF),
            ((2, tokens, 3 * pair), BF),
            ((2, n_blocks, pair // LANES, n_rows, 2 * n_rows), BF),
            ((2, frames, chunk, pair), BF),
            ((2, tokens, half), F32),
            ((2, tokens, half), BF),
        ],
        who, xo, xp, gain, wcat, wout, mask,
        name="attend_forward",
    )
    recv_f = exchange(send_f, "tensor", 2)

    pcot4, keep_b, send_b, stats, gains = call(
        functools.partial(backward_kernel, frames, rows),
        [
            ((2, frames, chunk, 3 * pair), BF),
            ((2, tokens, half), F32),
            ((2, tokens, half), BF),
            ((8, 2 * tokens), F32),
            ((1, width), F32),
        ],
        who, co, cp, packed, weights, normed, gain, wcat, wout,
        name="attend_backward",
    )
    recv_b = exchange(send_b, "tensor", 2)
    stats_in = exchange(stats, "tensor", 2)

    grad_keep, grad_send = call(
        grads_kernel,
        [((width, 4 * share), F32), ((width, 4 * share), BF)],
        normed, pcot4.reshape(2, tokens, 3 * pair), co, cp, mixed4.reshape(2, tokens, pair),
        scalars=0,
        name="weight_grads",
    )
    grads = grad_keep + exchange(grad_send, "tensor", 1).astype(F32)
    per = width // n_tm
    bit = 1
    while bit < n_tm:
        grads = grads.reshape(n_tm // (2 * bit), 2, per, 4 * share)
        mine = (k // bit) % 2
        out = lax.dynamic_index_in_dim(grads, 1 - mine, 1, keepdims=False).astype(BF)
        grads = lax.dynamic_index_in_dim(grads, mine, 1, keepdims=False)
        grads = grads + exchange(out, "tm", bit).astype(F32)
        bit *= 2
    grads = grads.reshape(per, 4 * share).astype(BF)
    grad_qkv = grads[:, : 3 * share].reshape(per, 3, share)
    grad_proj = grads[:, 3 * share :].T

    for bit in (2, 1):
        gains = gains + exchange(gains, "tensor", bit)
    bit = 1
    while bit < n_tm:
        gains = gains + exchange(gains, "tm", bit)
        bit *= 2
    grad_gain = lax.dynamic_slice_in_dim(gains.reshape(width), j * share, share, 0)

    pieces = ((2, tokens, share), BF)

    def return_to_frames(own, swap):
        recv = exchange(swap, "tensor", 1)
        (message,) = call(
            pack_kernel,
            [((frames, 2, chunk, 2 * share), BF)],
            own.reshape(2, frames, chunk, share), recv.reshape(2, frames, chunk, share),
            scalars=0,
            name="pack",
        )
        return lax.all_to_all(message, "tm", split_axis=0, concat_axis=0, tiled=True)

    first = return_to_frames(
        *call(finish_forward_kernel, [pieces, pieces], who, xo, xp, keep_f, recv_f, name="finish_f")
    )
    second = return_to_frames(
        *call(
            finish_backward_kernel, [pieces, pieces],
            who, xo, xp, co, cp, gain, keep_b, recv_b, stats, stats_in,
            name="finish_b",
        )
    )
    whole = ((n_tm, n_te, chunk, share), BF)
    block_out, grad_in = call(assemble_kernel, [whole, whole], who, first, second, name="assemble")
    block_out = block_out.reshape(1, place_total, share)
    grad_in = grad_in.reshape(1, place_total, share)
    return (block_out, grad_in, grad_qkv, grad_proj, grad_gain)


def solution(mesh):
    in_specs = (
        P("tm", None, None),
        P(),
        P(None, None, "tensor"),
        P("tensor", None),
        P(),
        P("tm", None, None),
    )
    out_specs = (
        P("tm", None, "tensor"),
        P("tm", None, "tensor"),
        P("tm", None, "tensor"),
        P("tensor", "tm"),
        P("tensor"),
    )
    return jax.shard_map(body, mesh=mesh, in_specs=in_specs, out_specs=out_specs, check_vma=False)
```

```python
import functools

import jax
import jax.numpy as jnp
from jax import lax
from jax.experimental import pallas as pl
from jax.experimental.pallas import tpu as pltpu
from jax.sharding import PartitionSpec as P

D = 768
H = 12
HEAD = D // H
LANES = 128
EPS = 1e-05
MASKED = -1000000000.0

BF = jnp.bfloat16
F32 = jnp.float32


def exchange(value, axis, bit):
    size = lax.axis_size(axis)
    return lax.ppermute(value, axis, [(i, i ^ bit) for i in range(size)])


def dot(a, b):
    return lax.dot_general(a, b, (((1,), (0,)), ((), ())), preferred_element_type=F32)


def dot_t(a, b):
    return lax.dot_general(a, b, (((1,), (1,)), ((), ())), preferred_element_type=F32)


def t_dot(a, b):
    return lax.dot_general(a, b, (((0,), (0,)), ((), ())), preferred_element_type=F32)


def standardize(x):
    x = x.astype(F32)
    shifted = x - jnp.mean(x, axis=-1, keepdims=True)
    inverse = lax.rsqrt(jnp.mean(shifted * shifted, axis=-1, keepdims=True) + EPS)
    return shifted * inverse, inverse


def block_rows(value, frames, b, rows):
    q = value.shape[0] // frames
    if q == rows:
        return value
    cut = value.reshape(frames, q, value.shape[1])[:, b * rows : (b + 1) * rows]
    return cut.reshape(frames * rows, value.shape[1])


def put_rows(ref, g, b, rows, col, value):
    frames = ref.shape[1]
    ref[g, :, b * rows : (b + 1) * rows, col : col + value.shape[1]] = value.reshape(
        frames, rows, value.shape[1]
    )


def split_heads(value):
    lane = lax.broadcasted_iota(jnp.int32, value.shape, 1)
    zero = jnp.zeros_like(value)
    return jnp.concatenate(
        [jnp.where(lane < HEAD, value, zero), jnp.where(lane >= HEAD, value, zero)], axis=0
    )


def join_heads(value):
    n = value.shape[0] // 2
    lane = lax.broadcasted_iota(jnp.int32, (n, value.shape[1]), 1)
    return jnp.where(lane < HEAD, value[:n], value[n:])


def all_rows(parts):
    return jnp.concatenate(list(parts), axis=0)


def weight_rows(own, other, which):
    return all_rows((own[which], other[which]))


def send_kernel(n_near, n_slots, k, j, source, *refs):
    outs, sems = refs[:n_slots], refs[n_slots]
    copies = []
    for s in range(n_slots):
        if s < n_near:
            for g in range(2):
                copies.append((source.at[k[0] ^ s, j[0] ^ (2 * g)], outs[s].at[g]))
        else:
            copies.append((source.at[k[0] ^ s, j[0]], outs[s]))
    started = [
        pltpu.make_async_copy(src, dst, sems.at[i]) for i, (src, dst) in enumerate(copies)
    ]
    for copy in started:
        copy.start()
    for copy in started:
        copy.wait()


def token_groups(refs, n_near, n_slots):
    near, far, passed = refs[:n_near], refs[n_near:n_slots], refs[n_slots:]
    first = [r[0] for r in near] + [r[...] for r in far]
    second = [r[1] for r in near] + [r[...] for r in passed]
    return all_rows(first), all_rows(second)


def forward_kernel(frames, rows, n_near, n_in, who, gain, wa, wb, oa, ob, mask, *refs):
    tokens_in = refs[:n_in]
    x_all, normed, packed, weights, mixed, keep, send = refs[n_in:]
    hi = who[0] // 2
    wq, wk, wv = (weight_rows(wa, wb, i) for i in range(3))
    wout = all_rows((oa[...], ob[...]))
    width, full = wout.shape
    half = full // 2
    for g, x in enumerate(token_groups(tokens_in, n_near, frames)):
        tokens = x.shape[0]
        x_all[g] = x
        standard, _ = standardize(x)
        n = (standard * gain[...]).astype(BF)
        normed[g] = n
        qs, ks, vs = (dot_t(n, w).astype(BF) for w in (wq, wk, wv))
        packed[g] = jnp.concatenate([qs, ks, vs], axis=1)
        for b in range(tokens // (frames * rows)):
            inside = mask[g, b]
            for p in range(width // LANES):
                cols = slice(p * LANES, (p + 1) * LANES)
                q, k, v = (block_rows(z[:, cols], frames, b, rows) for z in (qs, ks, vs))
                s = dot_t(q, split_heads(k)) * HEAD ** (-0.5)
                n_rows = frames * rows
                both = []
                for e in range(2):
                    part = jnp.where(inside > 0, s[:, e * n_rows : (e + 1) * n_rows], MASKED)
                    top = jnp.max(part, axis=-1, keepdims=True)
                    ex = jnp.exp(part - top) * inside
                    total = jnp.sum(ex, axis=-1, keepdims=True)
                    total = jnp.where(total > 0, total, 1.0)
                    both.append((ex / total).astype(BF))
                w = jnp.concatenate(both, axis=1)
                weights[g, b, p] = w
                put_rows(mixed, g, b, rows, p * LANES, dot(w, split_heads(v)).astype(BF))
        m = mixed[g].reshape(tokens, width)
        y = dot(m, wout)
        low, high = y[:, :half], y[:, half:]
        keep[g] = jnp.where(hi == 0, low, high)
        send[g] = jnp.where(hi == 0, high, low).astype(BF)


def backward_kernel(
    frames, rows, n_near, n_in, who, gain, wa, wb, oa, ob, packed, weights, normed, *refs
):
    tokens_in = refs[:n_in]
    c_all, pcot, keep, send, stats, gains = refs[n_in:]
    hi = who[0] // 2
    wq, wk, wv = (weight_rows(wa, wb, i) for i in range(3))
    wcat = all_rows((wq, wk, wv))
    wout = all_rows((oa[...], ob[...]))
    width, full = wout.shape
    half = full // 2
    total_gain = jnp.zeros((1, full), F32)
    for g, c in enumerate(token_groups(tokens_in, n_near, frames)):
        tokens = c.shape[0]
        c_all[g] = c
        mc = dot_t(c, wout).astype(BF)
        pk = packed[g]
        for b in range(tokens // (frames * rows)):
            for p in range(width // LANES):
                q, k, v = (
                    block_rows(pk[:, i * width + p * LANES : i * width + (p + 1) * LANES], frames, b, rows)
                    for i in range(3)
                )
                dm = block_rows(mc[:, p * LANES : (p + 1) * LANES], frames, b, rows)
                dw = dot_t(dm, split_heads(v)).astype(BF).astype(F32)
                w = weights[g, b, p]
                n_rows = frames * rows
                both = []
                for e in range(2):
                    we = w[:, e * n_rows : (e + 1) * n_rows].astype(F32)
                    de = dw[:, e * n_rows : (e + 1) * n_rows]
                    inner = jnp.sum(we * de, axis=-1, keepdims=True)
                    both.append((we * (de - inner) * HEAD ** (-0.5)).astype(BF))
                ds = jnp.concatenate(both, axis=1)
                dq = dot(ds, split_heads(k)).astype(BF)
                dk = join_heads(t_dot(ds, q)).astype(BF)
                dv = join_heads(t_dot(w, dm)).astype(BF)
                put_rows(pcot, g, b, rows, p * LANES, dq)
                put_rows(pcot, g, b, rows, width + p * LANES, dk)
                put_rows(pcot, g, b, rows, 2 * width + p * LANES, dv)
        pc = pcot[g].reshape(tokens, 3 * width)
        nc = dot(pc, wcat)
        nn = normed[g].astype(F32) * nc
        mean_plain = jnp.sum(nc * gain[...], axis=-1, keepdims=True)
        mean_cross = jnp.sum(nn, axis=-1, keepdims=True)
        total_gain = total_gain + jnp.sum(nn, axis=0, keepdims=True)
        lane = lax.broadcasted_iota(jnp.int32, (tokens, LANES), 1)
        both = jnp.where(lane == 0, mean_plain, mean_cross) * (1.0 / full)
        stats[:, g * tokens : (g + 1) * tokens] = both.T[:8]
        low, high = nc[:, :half], nc[:, half:]
        keep[g] = jnp.where(hi == 0, low, high)
        send[g] = jnp.where(hi == 0, high, low).astype(BF)
    total_gain = total_gain / gain[...]
    low, high = total_gain[:, :half], total_gain[:, half:]
    gains[...] = jnp.where(hi == 0, low, high)
    stats[2:3, :half] = jnp.where(hi == 0, high, low)


def grads_kernel(normed, pcot, c_all, mixed, keep, send):
    width = mixed.shape[2]
    share = width // 2
    columns = []
    for which in range(3):
        cols = slice(which * width, (which + 1) * width)
        columns.append(t_dot(normed[0], pcot[0][:, cols]) + t_dot(normed[1], pcot[1][:, cols]))
    columns.append(t_dot(c_all[0], mixed[0]) + t_dot(c_all[1], mixed[1]))
    keep[...] = jnp.concatenate([v[:, :share] for v in columns], axis=1)
    send[...] = jnp.concatenate([v[:, share:] for v in columns], axis=1).astype(BF)


def halves(value, who):
    half = value.shape[-1] // 2
    return jnp.where(who[0] // 2 == 0, value[..., :half], value[..., half:])


def own_and_other(value, who):
    share = value.shape[-1] // 2
    low, high = value[..., :share], value[..., share:]
    first = who[0] % 2 == 0
    return jnp.where(first, low, high), jnp.where(first, high, low)


def two_parts(value):
    top = value.astype(BF).astype(F32)
    return top, value - top


def finish_forward_kernel(who, x_all, keep, recv, own, swap):
    for g in range(2):
        tokens = x_all.shape[1]
        out = halves(x_all[g].astype(F32), who) + keep[g] + recv[1 - g].astype(F32)
        a, b = own_and_other(out, who)
        own[g] = a.astype(BF)
        swap[g * tokens : (g + 1) * tokens] = b.astype(BF)


def finish_backward_kernel(
    who, x_all, c_all, gain, keep, recv, stats, stats_in, gains, own, swap, own_gain
):
    tokens = x_all.shape[1]
    half = gains.shape[1]
    for g in range(2):
        standard, inverse = standardize(x_all[g])
        both = (
            stats[:, g * tokens : (g + 1) * tokens]
            + stats_in[:, (1 - g) * tokens : (2 - g) * tokens]
        ).T
        mean_plain, mean_cross = both[:, 0:1], both[:, 1:2]
        scaled = (keep[g] + recv[1 - g].astype(F32)) * halves(gain[...], who)
        through = inverse * (scaled - mean_plain - halves(standard, who) * mean_cross)
        out = halves(c_all[g].astype(F32), who) + through
        a, b = own_and_other(out, who)
        own[g] = a.astype(BF)
        swap[g * tokens : (g + 1) * tokens] = b.astype(BF)
    a, b = own_and_other(gains[...] + stats_in[2:3, :half], who)
    own_gain[...] = a
    top, rest = two_parts(b)
    row = lax.broadcasted_iota(jnp.int32, (16, b.shape[1]), 0)
    swap[2 * tokens :] = jnp.where(row == 0, top, jnp.where(row == 1, rest, 0.0)).astype(BF)


def pack_kernel(n_slots, who, own, recv, *refs):
    outs, held = refs[:n_slots], refs[n_slots]
    tokens = own.shape[1]
    chunk = tokens // n_slots
    share = own.shape[2]
    j = who[0]
    for s in range(n_slots):
        for g in range(2):
            rows = slice(s * chunk, (s + 1) * chunk)
            held[s, j ^ (2 * g)] = own[g, rows].astype(F32)
            held[s, j ^ (2 * g + 1)] = recv[g * tokens + s * chunk : g * tokens + (s + 1) * chunk].astype(F32)
        value = held[s].reshape(4 * chunk, share)
        outs[s][:share] = value.T.astype(BF)


def pack_gain_kernel(n_slots, who, own, recv, own_gain, *refs):
    pack_kernel(n_slots, who, own, recv, *refs)
    outs = refs[:n_slots]
    tokens = own.shape[1]
    share = own.shape[2]
    value = (
        own_gain[...]
        + recv[2 * tokens : 2 * tokens + 1].astype(F32)
        + recv[2 * tokens + 1 : 2 * tokens + 2].astype(F32)
    )
    lanes = outs[0].shape[1]
    n_parts = -(-share // lanes)
    rows = []
    for part in two_parts(value):
        if n_parts * lanes > share:
            part = jnp.concatenate([part, jnp.zeros((1, n_parts * lanes - share), F32)], axis=1)
        rows += [part[:, i * lanes : (i + 1) * lanes] for i in range(n_parts)]
    extra = outs[0].shape[0] - share
    block = jnp.zeros((extra, lanes), F32)
    at = lax.broadcasted_iota(jnp.int32, (extra, lanes), 0)
    for i, row in enumerate(rows):
        block = jnp.where(at == i, row, block)
    for out in outs:
        out[share:] = block.astype(BF)


def assemble_kernel(n_slots, k, *refs):
    parts, out = refs[:n_slots], refs[n_slots]
    share = out.shape[0]
    lanes = parts[0].shape[1]
    for s in range(n_slots):
        out[:, pl.ds(pl.multiple_of((k[0] ^ s) * lanes, lanes), lanes)] = parts[s][:share]


def assemble_gain_kernel(n_slots, k, *refs):
    assemble_kernel(n_slots, k, *refs)
    parts, out, total = refs[:n_slots], refs[n_slots], refs[n_slots + 1]
    share = out.shape[0]
    value = parts[0][share:].astype(F32)
    for s in range(1, n_slots):
        value = value + parts[s][share:].astype(F32)
    total[...] = value


def call(kernel, outs, *args, scalars=1, name=None, scratch=(), in_hbm=()):
    specs = []
    for i in range(len(args)):
        space = pltpu.SMEM if i < scalars else pl.ANY if i in in_hbm else pltpu.VMEM
        specs.append(pl.BlockSpec(memory_space=space))
    shapes = [jax.ShapeDtypeStruct(shape, kind) for shape, kind in outs]
    return pl.pallas_call(
        kernel,
        out_shape=shapes,
        in_specs=specs,
        out_specs=[pl.BlockSpec(memory_space=pltpu.VMEM)] * len(outs),
        scratch_shapes=scratch,
        name=name,
        compiler_params=pltpu.CompilerParams(vmem_limit_bytes=56 * 1024 * 1024),
    )(*args)


def body(frames_in, norm_gain, w_qkv, w_out, keep_runs, out_cotangent):
    _, place_total, width = frames_in.shape
    n_tm, n_te = lax.axis_size("tm"), lax.axis_size("tensor")
    frames = n_tm
    n_near = max(n_tm // 2, 1)
    chunk = place_total // (n_tm * n_te)
    tokens = frames * chunk
    rows = 16 if chunk % 16 == 0 else chunk
    k = lax.axis_index("tm").astype(jnp.int32)
    j = lax.axis_index("tensor").astype(jnp.int32)
    where, who = k.reshape(1), j.reshape(1)
    share = w_qkv.shape[2]
    pair = 2 * share
    half = width // 2

    def gather_positions(value, name):
        parts = call(
            functools.partial(send_kernel, n_near, n_tm),
            [((2, chunk, width), BF)] * n_near + [((chunk, width), BF)] * (n_tm - n_near),
            where, who, value.reshape(n_tm, n_te, chunk, width),
            scalars=2, in_hbm=(2,), name=name,
            scratch=[pltpu.SemaphoreType.DMA((n_tm + n_near,))],
        )
        far = [exchange(parts[s], "tm", s) for s in range(n_near, n_tm)]
        near = [parts[0]] + [exchange(parts[s], "tm", s) for s in range(1, n_near)]
        passed = [exchange(part, "tensor", 2) for part in far]
        return near + far + passed

    x_parts = gather_positions(frames_in, "send_x")
    c_parts = gather_positions(out_cotangent, "send_c")
    n_in = len(x_parts)

    w_own = jnp.transpose(w_qkv, (1, 2, 0))
    matrices = (w_own, exchange(w_own, "tensor", 1), w_out, exchange(w_out, "tensor", 1))
    gain = norm_gain.reshape(1, width)

    slot = jnp.arange(frames, dtype=jnp.int32)
    order = (slot[None, :] == (k ^ slot)[:, None]).astype(jnp.int32)
    runs = jnp.sum(order[:, :, None, None] * keep_runs[None], axis=1)
    starts = runs[:, :, 0]
    ends = starts + runs[:, :, 1]
    chunks = jnp.stack([j, j ^ 2])
    places = (
        k * (n_te * chunk) + chunks[:, None] * chunk + jnp.arange(chunk, dtype=jnp.int32)[None, :]
    )
    kept = jnp.any(
        (places[:, None, None, :] >= starts[None, :, :, None])
        & (places[:, None, None, :] < ends[None, :, :, None]),
        axis=2,
    )
    kept = kept.reshape(2, frames, chunk // rows, rows).transpose(0, 2, 1, 3)
    kept = kept.reshape(2, chunk // rows, frames * rows)
    place_of = jnp.arange(frames * rows, dtype=jnp.int32) % rows
    mask = (
        kept[:, :, :, None] & kept[:, :, None, :] & (place_of[:, None] == place_of[None, :])
    ).astype(F32)

    n_blocks = chunk // rows
    n_rows = frames * rows
    x_all, normed, packed, weights, mixed4, keep_f, send_f = call(
        functools.partial(forward_kernel, frames, rows, n_near, n_in),
        [
            ((2, tokens, width), BF),
            ((2, tokens, width), BF),
            ((2, tokens, 3 * pair), BF),
            ((2, n_blocks, pair // LANES, n_rows, 2 * n_rows), BF),
            ((2, frames, chunk, pair), BF),
            ((2, tokens, half), F32),
            ((2, tokens, half), BF),
        ],
        who, gain, *matrices, mask, *x_parts,
        name="attend_forward",
    )
    recv_f = exchange(send_f, "tensor", 2)

    c_all, pcot4, keep_b, send_b, stats, gains = call(
        functools.partial(backward_kernel, frames, rows, n_near, n_in),
        [
            ((2, tokens, width), BF),
            ((2, frames, chunk, 3 * pair), BF),
            ((2, tokens, half), F32),
            ((2, tokens, half), BF),
            ((8, 2 * tokens), F32),
            ((1, half), F32),
        ],
        who, gain, *matrices, packed, weights, normed, *c_parts,
        name="attend_backward",
    )
    recv_b = exchange(send_b, "tensor", 2)
    stats_in = exchange(stats, "tensor", 2)

    grad_keep, grad_send = call(
        grads_kernel,
        [((width, 4 * share), F32), ((width, 4 * share), BF)],
        normed, pcot4.reshape(2, tokens, 3 * pair), c_all, mixed4.reshape(2, tokens, pair),
        scalars=0,
        name="weight_grads",
    )
    grad_recv = exchange(grad_send, "tensor", 1)
    per = width // n_tm
    bits = [1 << i for i in range(n_tm.bit_length() - 1)]

    def reduce_over_tm(value, order):
        dims = [2] * len(bits)
        value = value.reshape(dims + list(value.shape[1:]))
        left = sorted(bits, reverse=True)
        for bit in order:
            axis = left.index(bit)
            mine = (k // bit) % 2
            out = lax.dynamic_index_in_dim(value, 1 - mine, axis, keepdims=False).astype(BF)
            value = lax.dynamic_index_in_dim(value, mine, axis, keepdims=False)
            value = value + exchange(out, "tm", bit).astype(F32)
            left.remove(bit)
        return value.reshape(per, value.shape[-1])

    orders = (bits, bits[1::-1] + bits[2:])
    column = 2 * share
    sums = []
    for i, order in enumerate(orders):
        cols = slice(i * column, (i + 1) * column)
        part = grad_keep[:, cols] + grad_recv[:, cols].astype(F32)
        sums.append(reduce_over_tm(part.reshape(n_tm, per, column), order).astype(BF))
    grad_qkv = jnp.stack(
        [sums[0][:, :share], sums[0][:, share:], sums[1][:, :share]], axis=1
    )
    grad_proj = sums[1][:, share:].T

    lanes = n_te * chunk
    n_parts = -(-share // lanes)
    gain_rows = -(-2 * n_parts // 16) * 16

    def return_to_frames(own, swap, *own_gain):
        recv = exchange(swap, "tensor", 1)
        extra = gain_rows if own_gain else 0
        messages = call(
            functools.partial(pack_gain_kernel if own_gain else pack_kernel, n_tm),
            [((share + extra, lanes), BF)] * n_tm,
            who, own, recv, *own_gain,
            name="pack", scratch=[pltpu.VMEM((n_tm, n_te, chunk, share), F32)],
        )
        back = [messages[0]] + [exchange(messages[s], "tm", s) for s in range(1, n_tm)]
        if lanes % LANES:
            whole = jnp.stack([back[0]] * n_tm)
            for s in range(n_tm):
                whole = lax.dynamic_update_index_in_dim(whole, back[s], k ^ s, 0)
            total = jnp.sum(whole[:, share:].astype(F32), axis=0)
            return jnp.transpose(whole[:, :share], (1, 0, 2)).reshape(share, place_total), total
        outs = [((share, place_total), BF)]
        if own_gain:
            outs.append(((gain_rows, lanes), F32))
        return call(
            functools.partial(assemble_gain_kernel if own_gain else assemble_kernel, n_tm),
            outs, where, *back, name="assemble",
        )

    mine = ((2, tokens, share), BF)
    own, swap = call(
        finish_forward_kernel, [mine, ((2 * tokens, share), BF)],
        who, x_all, keep_f, recv_f, name="finish_f",
    )
    block_out = return_to_frames(own, swap)[0]
    own, swap, own_gain = call(
        finish_backward_kernel,
        [mine, ((2 * tokens + 16, share), BF), ((1, share), F32)],
        who, x_all, c_all, gain, keep_b, recv_b, stats, stats_in, gains, name="finish_b",
    )
    grad_in, total = return_to_frames(own, swap, own_gain)
    grad_gain = (total[:n_parts] + total[n_parts : 2 * n_parts]).reshape(-1)[:share]
    return (block_out.T[None], grad_in.T[None], grad_qkv, grad_proj, grad_gain)


def solution(mesh):
    in_specs = (
        P("tm", None, None),
        P(),
        P(None, None, "tensor"),
        P("tensor", None),
        P(),
        P("tm", None, None),
    )
    out_specs = (
        P("tm", None, "tensor"),
        P("tm", None, "tensor"),
        P("tm", None, "tensor"),
        P("tensor", "tm"),
        P("tensor"),
    )
    return jax.shard_map(body, mesh=mesh, in_specs=in_specs, out_specs=out_specs, check_vma=False)
```

```python
import functools

import jax
import jax.numpy as jnp
from jax import lax
from jax.experimental import pallas as pl
from jax.experimental.pallas import tpu as pltpu
from jax.sharding import PartitionSpec as P

D = 768
H = 12
HEAD = D // H
LANES = 128
EPS = 1e-05
MASKED = -1000000000.0

BF = jnp.bfloat16
F32 = jnp.float32
VMEM_LIMIT = 16 * 1024 * 1024


def exchange(value, axis, bit):
    size = lax.axis_size(axis)
    return lax.ppermute(value, axis, [(i, i ^ bit) for i in range(size)])


def dot(a, b):
    return lax.dot_general(a, b, (((1,), (0,)), ((), ())), preferred_element_type=F32)


def dot_t(a, b):
    return lax.dot_general(a, b, (((1,), (1,)), ((), ())), preferred_element_type=F32)


def t_dot(a, b):
    return lax.dot_general(a, b, (((0,), (0,)), ((), ())), preferred_element_type=F32)


def standardize(x):
    x = x.astype(F32)
    shifted = x - jnp.mean(x, axis=-1, keepdims=True)
    inverse = lax.rsqrt(jnp.mean(shifted * shifted, axis=-1, keepdims=True) + EPS)
    return shifted * inverse, inverse


def block_rows(value, frames, b, rows):
    q = value.shape[0] // frames
    if q == rows:
        return value
    cut = value.reshape(frames, q, value.shape[1])[:, b * rows : (b + 1) * rows]
    return cut.reshape(frames * rows, value.shape[1])


def split_heads(value):
    lane = lax.broadcasted_iota(jnp.int32, value.shape, 1)
    zero = jnp.zeros_like(value)
    return jnp.concatenate(
        [jnp.where(lane < HEAD, value, zero), jnp.where(lane >= HEAD, value, zero)], axis=0
    )


def join_heads(value):
    n = value.shape[0] // 2
    lane = lax.broadcasted_iota(jnp.int32, (n, value.shape[1]), 1)
    return jnp.where(lane < HEAD, value[:n], value[n:])


def put_rows(ref, b, rows, col, value):
    ref[:, b * rows : (b + 1) * rows, col : col + value.shape[1]] = value.reshape(
        ref.shape[0], rows, value.shape[1]
    )


def all_rows(parts):
    return jnp.concatenate(list(parts), axis=0)


def halves(value, who):
    half = value.shape[-1] // 2
    low, high = value[..., :half], value[..., half:]
    first = who[0] // 2 == 0
    return jnp.where(first, low, high), jnp.where(first, high, low)


def own_and_other(value, who):
    share = value.shape[-1] // 2
    low, high = value[..., :share], value[..., share:]
    first = who[0] % 2 == 0
    return jnp.where(first, low, high), jnp.where(first, high, low)


def two_parts(value):
    top = value.astype(BF).astype(F32)
    return top, value - top


def send_kernel(n_near, n_slots, k, j, source, *refs):
    outs, sems = refs[:n_slots], refs[n_slots]
    copies = []
    for s in range(n_slots):
        if s < n_near:
            for g in range(2):
                copies.append((source.at[k[0] ^ s, j[0] ^ (2 * g)], outs[s].at[g]))
        else:
            copies.append((source.at[k[0] ^ s, j[0]], outs[s]))
    started = [
        pltpu.make_async_copy(src, dst, sems.at[i]) for i, (src, dst) in enumerate(copies)
    ]
    for copy in started:
        copy.start()
    for copy in started:
        copy.wait()


def attend_kernel(
    frames, rows, picks, who, where, gain, wa, wb, oa, ob, mask, x_in, *refs
):
    c_in = refs[: len(picks)]
    c_all, normed, mixed, pcot, keep, send, stats, gains = refs[len(picks) :]
    for s, (ref, pick) in enumerate(zip(c_in, picks)):
        if len(picks) == 1:
            c_all[...] = ref[...]
        else:
            c_all[where[0] ^ s] = ref[...] if pick is None else ref[pick]
    wq, wk, wv = (all_rows((wa[i], wb[i])) for i in range(3))
    wout = all_rows((oa[...], ob[...]))
    width, full = wout.shape
    chunk = x_in.shape[1]
    tokens = frames * chunk
    n_rows = frames * rows
    standard, _ = standardize(x_in[...].reshape(tokens, full))
    n = (standard * gain[...]).astype(BF)
    normed[...] = n
    qs, ks, vs = (dot_t(n, w).astype(BF) for w in (wq, wk, wv))
    c = c_all[...].reshape(tokens, full)
    mc = dot_t(c, wout).astype(BF)
    for b in range(chunk // rows):
        inside = mask[b]
        for p in range(width // LANES):
            cols = slice(p * LANES, (p + 1) * LANES)
            q, k, v, dm = (block_rows(z[:, cols], frames, b, rows) for z in (qs, ks, vs, mc))
            kk, vv = split_heads(k), split_heads(v)
            s = dot_t(q, kk) * HEAD ** (-0.5)
            dw = dot_t(dm, vv).astype(BF).astype(F32)
            w_parts, d_parts = [], []
            for e in range(2):
                part = jnp.where(inside > 0, s[:, e * n_rows : (e + 1) * n_rows], MASKED)
                top = jnp.max(part, axis=-1, keepdims=True)
                ex = jnp.exp(part - top) * inside
                total = jnp.sum(ex, axis=-1, keepdims=True)
                we = ex / jnp.where(total > 0, total, 1.0)
                de = dw[:, e * n_rows : (e + 1) * n_rows]
                inner = jnp.sum(we * de, axis=-1, keepdims=True)
                w_parts.append(we.astype(BF))
                d_parts.append((we * (de - inner) * HEAD ** (-0.5)).astype(BF))
            w = jnp.concatenate(w_parts, axis=1)
            ds = jnp.concatenate(d_parts, axis=1)
            put_rows(mixed, b, rows, p * LANES, dot(w, vv).astype(BF))
            put_rows(pcot, b, rows, p * LANES, dot(ds, kk).astype(BF))
            put_rows(pcot, b, rows, width + p * LANES, join_heads(t_dot(ds, q)).astype(BF))
            put_rows(pcot, b, rows, 2 * width + p * LANES, join_heads(t_dot(w, dm)).astype(BF))
    y = dot(mixed[...].reshape(tokens, width), wout)
    mine, other = halves(y, who)
    keep[0] = mine
    send[0] = other.astype(BF)
    pc = pcot[...].reshape(tokens, 3 * width)
    nc = dot(pc, all_rows((wq, wk, wv)))
    nn = n.astype(F32) * nc
    mean_plain = jnp.sum(nc * gain[...], axis=-1, keepdims=True)
    mean_cross = jnp.sum(nn, axis=-1, keepdims=True)
    total_gain = jnp.sum(nn, axis=0, keepdims=True) / gain[...]
    lane = lax.broadcasted_iota(jnp.int32, (tokens, LANES), 1)
    both = jnp.where(lane == 0, mean_plain, mean_cross) * (1.0 / full)
    half = full // 2
    stats[:, :tokens] = both.T[:8]
    mine, other = halves(nc, who)
    keep[1] = mine
    send[1] = other.astype(BF)
    mine, other = halves(total_gain, who)
    gains[...] = mine
    stats[:1, tokens : tokens + half] = other


def grads_kernel(n0, n1, p0, p1, c0, c1, m0, m1, keep, send):
    width = m0.shape[1]
    share = width // 2
    columns = []
    for which in range(3):
        cols = slice(which * width, (which + 1) * width)
        columns.append(t_dot(n0[...], p0[:, cols]) + t_dot(n1[...], p1[:, cols]))
    columns.append(t_dot(c0[...], m0[...]) + t_dot(c1[...], m1[...]))
    keep[...] = jnp.concatenate([v[:, :share] for v in columns], axis=1)
    send[...] = jnp.concatenate([v[:, share:] for v in columns], axis=1).astype(BF)


def halve_kernel(n_blocks, orders, step, n_held, where, *refs):
    held, moved, outs = refs[:n_held], refs[n_held : 2 * n_held], refs[2 * n_held :]
    k = where[0]
    for i, order in enumerate(orders):
        column = outs[2 * i].shape[-1]
        cols = slice(i * column, (i + 1) * column) if n_held == 1 else slice(None)
        keep, send = outs[2 * i : 2 * i + 2]
        source, came = held[i % n_held], moved[i % n_held]
        left = [bit for bit in (1 << b for b in range(n_blocks.bit_length())) if bit < n_blocks]
        left = [bit for bit in left if bit not in order[:step]]
        here = left.index(order[step])
        mine = (k // order[step]) % 2
        for n in range(keep.shape[0]):
            low = n % (1 << here)
            base = ((n >> here) << (here + 1)) + low
            stay = base + (mine << here)
            leave = base + ((1 - mine) << here)
            keep[n] = source[stay, :, cols] + came[stay, :, cols].astype(F32)
            send[n] = (source[leave, :, cols] + came[leave, :, cols].astype(F32)).astype(BF)


def last_grads_kernel(held_a, held_b, moved_a, moved_b, qkv, proj):
    share = proj.shape[0]
    a = held_a[0] + moved_a[0].astype(F32)
    b = held_b[0] + moved_b[0].astype(F32)
    qkv[0] = a[:, :share].astype(BF)
    qkv[1] = a[:, share:].astype(BF)
    qkv[2] = b[:, :share].astype(BF)
    proj[...] = b[:, share:].T.astype(BF)


def finish_kernel(who, x_in, c_in, gain, keep, recv, stats, stats_in, *refs):
    tokens = keep.shape[1]
    full = x_in.shape[-1]
    own, swap = refs[-2:] if len(refs) == 2 else refs[3:5]
    x = x_in[...].reshape(tokens, full)
    standard, inverse = standardize(x)
    both = (stats[:, :tokens] + stats_in[:, :tokens]).T
    mean_plain, mean_cross = both[:, 0:1], both[:, 1:2]
    out = halves(x.astype(F32), who)[0] + keep[0] + recv[0].astype(F32)
    scaled = (keep[1] + recv[1].astype(F32)) * halves(gain[...], who)[0]
    through = inverse * (scaled - mean_plain - halves(standard, who)[0] * mean_cross)
    back = halves(c_in[...].reshape(tokens, full).astype(F32), who)[0] + through
    for i, value in enumerate((out, back)):
        a, b = own_and_other(value, who)
        own[i] = a.astype(BF)
        swap[i * tokens : (i + 1) * tokens] = b.astype(BF)
    if len(refs) > 2:
        gains_a, gains_b, stats_other = refs[:3]
        own_gain = refs[5]
        half = full // 2
        sent = stats_in[:1, tokens : tokens + half] + stats_other[:1, tokens : tokens + half]
        a, b = own_and_other(gains_a[...] + gains_b[...] + sent, who)
        own_gain[...] = a
        top, rest = two_parts(b)
        row = lax.broadcasted_iota(jnp.int32, (16, b.shape[1]), 0)
        swap[2 * tokens :] = jnp.where(row == 0, top, jnp.where(row == 1, rest, 0.0)).astype(BF)


def pack_kernel(frames, who, own_a, own_b, recv_a, recv_b, own_gain, out, held):
    tokens, share = own_a.shape[1:]
    chunk = tokens // frames
    j = who[0]
    top = recv_a[2 * tokens : 2 * tokens + 2].astype(F32)
    value = own_gain[...] + top[:1] + top[1:]
    lanes = out.shape[2]
    n_parts = -(-share // lanes)
    extra = out.shape[1] - 2 * share
    block = jnp.zeros((extra, lanes), F32)
    at = lax.broadcasted_iota(jnp.int32, (extra, lanes), 0)
    row = 0
    for part in two_parts(value):
        if n_parts * lanes > share:
            part = jnp.concatenate([part, jnp.zeros((1, n_parts * lanes - share), F32)], axis=1)
        for i in range(n_parts):
            block = jnp.where(at == row, part[:, i * lanes : (i + 1) * lanes], block)
            row += 1
    for i in range(2):
        for s in range(frames):
            rows = slice(s * chunk, (s + 1) * chunk)
            sent = slice(i * tokens + s * chunk, i * tokens + (s + 1) * chunk)
            held[i, s, j] = own_a[i, rows].astype(F32)
            held[i, s, j ^ 2] = own_b[i, rows].astype(F32)
            held[i, s, j ^ 1] = recv_a[sent].astype(F32)
            held[i, s, j ^ 3] = recv_b[sent].astype(F32)
            turned = held[i, s].reshape(4 * chunk, share).T.astype(BF)
            out[s, i * share : (i + 1) * share] = turned
    for s in range(frames):
        out[s, 2 * share :] = block.astype(BF)


def assemble_kernel(parts, first, second, total, held, sems):
    n_slots, rows, lanes = parts.shape
    share = first.shape[0]
    copies = []
    for i, out in enumerate((first, second)):
        for s in range(n_slots):
            copies.append(
                pltpu.make_async_copy(
                    parts.at[s, pl.ds(i * share, share)],
                    out.at[:, pl.ds(s * lanes, lanes)],
                    sems.at[i * n_slots + s],
                )
            )
    copies.append(
        pltpu.make_async_copy(
            parts.at[:, pl.ds(2 * share, rows - 2 * share)], held, sems.at[2 * n_slots]
        )
    )
    for copy in copies:
        copy.start()
    for copy in copies:
        copy.wait()
    value = held[0].astype(F32)
    for s in range(1, n_slots):
        value = value + held[s].astype(F32)
    total[...] = value


def call(kernel, outs, *args, scalars=1, scratch=(), in_hbm=(), out_hbm=()):
    def space(i, hbm):
        return pl.BlockSpec(memory_space=pl.ANY if i in hbm else pltpu.VMEM)

    return pl.pallas_call(
        kernel,
        out_shape=[jax.ShapeDtypeStruct(shape, kind) for shape, kind in outs],
        in_specs=[pl.BlockSpec(memory_space=pltpu.SMEM)] * scalars
        + [space(i, in_hbm) for i in range(scalars, len(args))],
        out_specs=[space(i, out_hbm) for i in range(len(outs))],
        scratch_shapes=scratch,
        compiler_params=pltpu.CompilerParams(vmem_limit_bytes=VMEM_LIMIT),
    )(*args)


def block(frames_in, norm_gain, w_qkv, w_out, keep_runs, out_cotangent):
    _, place_total, width = frames_in.shape
    n_tm, n_te = lax.axis_size("tm"), lax.axis_size("tensor")
    frames = n_tm
    direct = n_tm <= 8
    n_near = n_tm // 2
    chunk = place_total // (n_tm * n_te)
    tokens = frames * chunk
    rows = 16 if chunk % 16 == 0 else chunk
    k = lax.axis_index("tm").astype(jnp.int32)
    j = lax.axis_index("tensor").astype(jnp.int32)
    where, who = k.reshape(1), j.reshape(1)
    share = w_qkv.shape[2]
    pair = 2 * share
    half = width // 2
    lanes = n_te * chunk

    w_own = jnp.transpose(w_qkv, (1, 2, 0))
    matrices = (w_own, exchange(w_own, "tensor", 1), w_out, exchange(w_out, "tensor", 1))
    gain = norm_gain.reshape(1, width)

    def gather_chunks(value):
        mine = lax.dynamic_index_in_dim(
            value.reshape(n_tm, n_te, chunk, width), j, 1, keepdims=False
        )
        first = lax.all_to_all(mine, "tm", split_axis=0, concat_axis=0, tiled=True)
        return first, exchange(first, "tensor", 2)

    xs = gather_chunks(frames_in)
    if direct:
        parts = call(
            functools.partial(send_kernel, n_near, n_tm),
            [((2, chunk, width), BF)] * n_near + [((chunk, width), BF)] * (n_tm - n_near),
            where, who, out_cotangent.reshape(n_tm, n_te, chunk, width),
            scalars=2, in_hbm=(2,), out_hbm=range(n_tm),
            scratch=[pltpu.SemaphoreType.DMA((n_tm + n_near,))],
        )
        far = [exchange(parts[s], "tm", s) for s in range(n_near, n_tm)]
        near = [parts[0]] + [exchange(parts[s], "tm", s) for s in range(1, n_near)]
        passed = [exchange(part, "tensor", 2) for part in far]
        cs = (near + far, near + passed)
        picks = [[g] * n_near + [None] * (n_tm - n_near) for g in range(2)]
    else:
        cs = tuple([value] for value in gather_chunks(out_cotangent))
        picks = [[None], [None]]

    starts = keep_runs[:, :, 0]
    ends = starts + keep_runs[:, :, 1]
    chunks = jnp.stack([j, j ^ 2])
    places = (
        k * (n_te * chunk) + chunks[:, None] * chunk + jnp.arange(chunk, dtype=jnp.int32)[None, :]
    )
    kept = jnp.any(
        (places[:, None, None, :] >= starts[None, :, :, None])
        & (places[:, None, None, :] < ends[None, :, :, None]),
        axis=2,
    )
    kept = kept.reshape(2, frames, chunk // rows, rows).transpose(0, 2, 1, 3)
    kept = kept.reshape(2, chunk // rows, frames * rows)
    place_of = jnp.arange(frames * rows, dtype=jnp.int32) % rows
    mask = (
        kept[:, :, :, None] & kept[:, :, None, :] & (place_of[:, None] == place_of[None, :])
    ).astype(F32)

    cube = (frames, chunk)
    done, recvs, stats_in = [], [], []
    for g in range(2):
        done.append(
            call(
                functools.partial(attend_kernel, frames, rows, picks[g]),
                [
                    (cube + (width,), BF),
                    ((tokens, width), BF),
                    (cube + (pair,), BF),
                    (cube + (3 * pair,), BF),
                    ((2, tokens, half), F32),
                    ((2, tokens, half), BF),
                    ((8, tokens + -(-half // LANES) * LANES), F32),
                    ((1, half), F32),
                ],
                who, where, gain, *matrices, mask[g], xs[g], *cs[g],
                scalars=2,
            )
        )
        recvs.append(exchange(done[g][5], "tensor", 2))
        stats_in.append(exchange(done[g][6], "tensor", 2))

    flat = lambda value: value.reshape(tokens, value.shape[-1])
    grad_keep, grad_send = call(
        grads_kernel,
        [((width, 4 * share), F32), ((width, 4 * share), BF)],
        done[0][1], done[1][1], flat(done[0][3]), flat(done[1][3]),
        flat(done[0][0]), flat(done[1][0]), flat(done[0][2]), flat(done[1][2]),
        scalars=0,
    )
    grad_recv = exchange(grad_send, "tensor", 1)
    per = width // n_tm
    bits = [1 << i for i in range(n_tm.bit_length() - 1)]
    column = 2 * share
    orders = (bits, bits[1::-1] + bits[2:])
    held = [grad_keep.reshape(n_tm, per, 4 * share)]
    moved = [grad_recv.reshape(n_tm, per, 4 * share)]
    for step in range(len(bits)):
        count = n_tm >> (step + 1)
        piece = (count, per, column)
        result = call(
            functools.partial(halve_kernel, n_tm, orders, step, len(held)),
            [(piece, F32), (piece, BF)] * 2,
            where, *held, *moved,
        )
        held = [result[0], result[2]]
        moved = [exchange(result[2 * i + 1], "tm", orders[i][step]) for i in range(2)]
    grad_qkv, grad_proj = call(
        last_grads_kernel,
        [((3, per, share), BF), ((share, per), BF)],
        *held, *moved,
        scalars=0,
    )
    grad_qkv = jnp.transpose(grad_qkv, (1, 0, 2))

    owns, swapped = [None, None], [None, None]
    for g in (1, 0):
        c_all, _, _, _, keep, _, stats, gains = done[g]
        outs = [((2, tokens, share), BF), ((2 * tokens + (0 if g else 16), share), BF)]
        more = ()
        if g == 0:
            outs.append(((1, share), F32))
            more = (gains, done[1][7], stats_in[0])
        result = call(
            finish_kernel, outs,
            who, xs[g], c_all, gain, keep, recvs[1 - g], stats, stats_in[1 - g], *more,
        )
        owns[g], swap = result[:2]
        swapped[g] = exchange(swap, "tensor", 1)
        if g == 0:
            own_gain = result[2]

    if direct:
        n_parts = -(-share // lanes)
        extra = -(-2 * n_parts // 16) * 16
        (message,) = call(
            functools.partial(pack_kernel, frames),
            [((frames, 2 * share + extra, lanes), BF)],
            who, *owns, *swapped, own_gain,
            scratch=[pltpu.VMEM((2, frames, n_te, chunk, share), F32)],
        )
        message = lax.all_to_all(message, "tm", split_axis=0, concat_axis=0, tiled=True)
        whole = ((share, place_total), BF)
        block_out, grad_in, total = call(
            assemble_kernel, [whole, whole, ((extra, lanes), F32)], message,
            scalars=0, in_hbm=(0,), out_hbm=(0, 1),
            scratch=[
                pltpu.VMEM((n_tm, extra, lanes), BF),
                pltpu.SemaphoreType.DMA((2 * n_tm + 1,)),
            ],
        )
        block_out, grad_in = block_out.T, grad_in.T
        grad_gain = (total[:n_parts] + total[n_parts : 2 * n_parts]).reshape(-1)[:share]
    else:
        order = jnp.arange(n_te, dtype=jnp.int32) ^ j
        four = jnp.stack(
            [owns[0], swapped[0][: 2 * tokens].reshape(2, tokens, share),
             owns[1], swapped[1].reshape(2, tokens, share)]
        )[order].reshape(n_te, 2, frames, chunk, share)
        message = jnp.transpose(four, (2, 1, 0, 3, 4)).reshape(frames, 2, lanes, share)
        message = lax.all_to_all(message, "tm", split_axis=0, concat_axis=0, tiled=True)
        block_out = message[:, 0].reshape(place_total, share)
        grad_in = message[:, 1].reshape(place_total, share)
        sent = swapped[0][2 * tokens : 2 * tokens + 2].astype(F32)
        grad_gain = lax.psum(own_gain[0] + sent[0] + sent[1], "tm")
    return (block_out[None], grad_in[None], grad_qkv, grad_proj, grad_gain)


def solution(mesh):
    in_specs = (
        P("tm", None, None),
        P(),
        P(None, None, "tensor"),
        P("tensor", None),
        P(),
        P("tm", None, None),
    )
    out_specs = (
        P("tm", None, "tensor"),
        P("tm", None, "tensor"),
        P("tm", None, "tensor"),
        P("tensor", "tm"),
        P("tensor"),
    )
    return jax.shard_map(block, mesh=mesh, in_specs=in_specs, out_specs=out_specs, check_vma=False)
```

```python
import functools

import jax
import jax.numpy as jnp
from jax import lax
from jax.experimental import pallas as pl
from jax.experimental.pallas import tpu as pltpu
from jax.sharding import PartitionSpec as P

D = 768
H = 12
HEAD = D // H
LANES = 128
EPS = 1e-05
MASKED = -1000000000.0

BF = jnp.bfloat16
F32 = jnp.float32
VMEM_LIMIT = 12 * 1024 * 1024
WHOLE_VMEM = 61*1024*1024


def exchange(value, axis, bit):
    size = lax.axis_size(axis)
    return lax.ppermute(value, axis, [(i, i ^ bit) for i in range(size)])


def dot(a, b):
    return lax.dot_general(a, b, (((1,), (0,)), ((), ())), preferred_element_type=F32)


def dot_t(a, b):
    return lax.dot_general(a, b, (((1,), (1,)), ((), ())), preferred_element_type=F32)


def t_dot(a, b):
    return lax.dot_general(a, b, (((0,), (0,)), ((), ())), preferred_element_type=F32)


def standardize(x):
    x = x.astype(F32)
    shifted = x - jnp.mean(x, axis=-1, keepdims=True)
    inverse = lax.rsqrt(jnp.mean(shifted * shifted, axis=-1, keepdims=True) + EPS)
    return shifted * inverse, inverse


def block_rows(value, frames, b, rows):
    q = value.shape[0] // frames
    if q == rows:
        return value
    cut = value.reshape(frames, q, value.shape[1])[:, b * rows : (b + 1) * rows]
    return cut.reshape(frames * rows, value.shape[1])


def split_heads(value):
    lane = lax.broadcasted_iota(jnp.int32, value.shape, 1)
    zero = jnp.zeros_like(value)
    return jnp.concatenate(
        [jnp.where(lane < HEAD, value, zero), jnp.where(lane >= HEAD, value, zero)], axis=0
    )


def join_heads(value):
    n = value.shape[0] // 2
    lane = lax.broadcasted_iota(jnp.int32, (n, value.shape[1]), 1)
    return jnp.where(lane < HEAD, value[:n], value[n:])


def put_rows(ref, b, rows, col, value):
    ref[:, b * rows : (b + 1) * rows, col : col + value.shape[1]] = value.reshape(
        ref.shape[0], rows, value.shape[1]
    )


def all_rows(parts):
    return jnp.concatenate(list(parts), axis=0)


def halves(value, who):
    half = value.shape[-1] // 2
    low, high = value[..., :half], value[..., half:]
    first = who[0] // 2 == 0
    return jnp.where(first, low, high), jnp.where(first, high, low)


def own_and_other(value, who):
    share = value.shape[-1] // 2
    low, high = value[..., :share], value[..., share:]
    first = who[0] % 2 == 0
    return jnp.where(first, low, high), jnp.where(first, high, low)


def two_parts(value):
    top = value.astype(BF).astype(F32)
    return top, value - top


def copy_all(pairs, sems):
    copies = [pltpu.make_async_copy(src, dst, sems.at[i]) for i, (src, dst) in enumerate(pairs)]
    for copy in copies:
        copy.start()
    for copy in copies:
        copy.wait()


def send_x_kernel(j, x_in, x_out, sems):
    copy_all([(x_in.at[i, j[0]], x_out.at[i]) for i in range(x_out.shape[0])], sems)


def send_c_kernel(n_near, n_slots, k, j, c_in, *refs):
    outs, sems = refs[:n_slots], refs[n_slots]
    pairs = []
    for s in range(n_slots):
        if s < n_near:
            for g in range(2):
                pairs.append((c_in.at[k[0] ^ s, j[0] ^ (2 * g)], outs[s].at[g]))
        else:
            pairs.append((c_in.at[k[0] ^ s, j[0]], outs[s]))
    copy_all(pairs, sems)


def stack_kernel(*refs):
    parts, out = refs[:-1], refs[-1]
    for i, ref in enumerate(parts):
        out[i] = ref[...]


def kept_row(runs, frames, rows, first):
    lane = lax.broadcasted_iota(jnp.int32, (frames, frames * rows), 1)
    frame = lax.broadcasted_iota(jnp.int32, (frames, frames * rows), 0)
    place = first + lane % rows
    begins, lengths = runs[:, 0, :], runs[:, 1, :]
    hits = jnp.zeros((frames, frames * rows), F32)
    for r in range(begins.shape[1]):
        begin = begins[:, r : r + 1]
        here = (place >= begin) & (place < begin + lengths[:, r : r + 1])
        hits = jnp.where(here, 1.0, hits)
    return jnp.sum(jnp.where(frame == lane // rows, hits, 0.0), axis=0, keepdims=True)


def attend_kernel(
    frames, rows, picks, n_te, g, who, where, gain_in, wa, wb, oa, ob, runs, x_in, *refs
):
    c_in, rest = refs[: len(picks)], refs[len(picks) :]
    c_all, normed, mixed, pcot, keep, send, stats, gains = rest
    if len(picks) == 1:
        c_all[...] = c_in[0][...]
    else:
        for s, (ref, pick) in enumerate(zip(c_in, picks)):
            c_all[where[0] ^ s] = ref[...] if pick is None else ref[pick]
    gain = gain_in[...].reshape(1, x_in.shape[2])
    wq, wk, wv = (all_rows((wa[i], wb[i])) for i in range(3))
    wout = all_rows((oa[...], ob[...]))
    width, full = wout.shape
    chunk = x_in.shape[1]
    tokens = frames * chunk
    n_rows = frames * rows
    standard, _ = standardize(x_in[...].reshape(tokens, full))
    n = (standard * gain).astype(BF)
    normed[...] = n
    qs, ks, vs = (dot_t(n, w).astype(BF) for w in (wq, wk, wv))
    c = c_all[...].reshape(tokens, full)
    mc = dot_t(c, wout).astype(BF)
    row = lax.broadcasted_iota(jnp.int32, (n_rows, n_rows), 0)
    col = lax.broadcasted_iota(jnp.int32, (n_rows, n_rows), 1)
    first = (where[0] * n_te + (who[0] ^ (2 * g))) * chunk
    for b in range(chunk // rows):
        across = kept_row(runs, frames, rows, first + b * rows)
        down = jnp.sum(jnp.where(row == col, across, 0.0), axis=1, keepdims=True)
        inside = jnp.where(row % rows == col % rows, across * down, 0.0)
        for p in range(width // LANES):
            cols = slice(p * LANES, (p + 1) * LANES)
            q, k, v, dm = (block_rows(z[:, cols], frames, b, rows) for z in (qs, ks, vs, mc))
            kk, vv = split_heads(k), split_heads(v)
            s = dot_t(q, kk) * HEAD ** (-0.5)
            dw = dot_t(dm, vv).astype(BF).astype(F32)
            w_parts, d_parts = [], []
            for e in range(2):
                part = jnp.where(inside > 0, s[:, e * n_rows : (e + 1) * n_rows], MASKED)
                top = jnp.max(part, axis=-1, keepdims=True)
                ex = jnp.exp(part - top) * inside
                total = jnp.sum(ex, axis=-1, keepdims=True)
                we = ex / jnp.where(total > 0, total, 1.0)
                de = dw[:, e * n_rows : (e + 1) * n_rows]
                inner = jnp.sum(we * de, axis=-1, keepdims=True)
                w_parts.append(we.astype(BF))
                d_parts.append((we * (de - inner) * HEAD ** (-0.5)).astype(BF))
            w = jnp.concatenate(w_parts, axis=1)
            ds = jnp.concatenate(d_parts, axis=1)
            put_rows(mixed, b, rows, p * LANES, dot(w, vv).astype(BF))
            put_rows(pcot, b, rows, p * LANES, dot(ds, kk).astype(BF))
            put_rows(pcot, b, rows, width + p * LANES, join_heads(t_dot(ds, q)).astype(BF))
            put_rows(pcot, b, rows, 2 * width + p * LANES, join_heads(t_dot(w, dm)).astype(BF))
    y = dot(mixed[...].reshape(tokens, width), wout)
    mine, other = halves(y, who)
    keep[0] = mine
    send[0] = other.astype(BF)
    pc = pcot[...].reshape(tokens, 3 * width)
    nc = dot(pc, all_rows((wq, wk, wv)))
    nn = n.astype(F32) * nc
    mean_plain = jnp.sum(nc * gain, axis=-1, keepdims=True)
    mean_cross = jnp.sum(nn, axis=-1, keepdims=True)
    total_gain = jnp.sum(nn, axis=0, keepdims=True) / gain
    lane = lax.broadcasted_iota(jnp.int32, (tokens, LANES), 1)
    both = jnp.where(lane == 0, mean_plain, mean_cross) * (1.0 / full)
    half = full // 2
    stats[:, :tokens] = both.T[:8]
    mine, other = halves(nc, who)
    keep[1] = mine
    send[1] = other.astype(BF)
    mine, other = halves(total_gain, who)
    gains[...] = mine
    stats[:1, tokens : tokens + half] = other


def grads_kernel(n0, n1, p0, p1, c0, c1, m0, m1, keep, send):
    width = m0.shape[1]
    share = width // 2
    columns = []
    for which in range(3):
        cols = slice(which * width, (which + 1) * width)
        columns.append(t_dot(n0[...], p0[:, cols]) + t_dot(n1[...], p1[:, cols]))
    columns.append(t_dot(c0[...], m0[...]) + t_dot(c1[...], m1[...]))
    keep[...] = jnp.concatenate([v[:, :share] for v in columns], axis=1)
    send[...] = jnp.concatenate([v[:, share:] for v in columns], axis=1).astype(BF)


def halve_kernel(n_blocks, orders, step, n_held, where, *refs):
    held, moved, outs = refs[:n_held], refs[n_held : 2 * n_held], refs[2 * n_held :]
    k = where[0]
    for i, order in enumerate(orders):
        column = outs[2 * i].shape[-1]
        cols = slice(i * column, (i + 1) * column) if n_held == 1 else slice(None)
        keep, send = outs[2 * i : 2 * i + 2]
        source, came = held[i % n_held], moved[i % n_held]
        left = [bit for bit in (1 << b for b in range(n_blocks.bit_length())) if bit < n_blocks]
        left = [bit for bit in left if bit not in order[:step]]
        here = left.index(order[step])
        mine = (k // order[step]) % 2
        for n in range(keep.shape[0]):
            low = n % (1 << here)
            base = ((n >> here) << (here + 1)) + low
            stay = base + (mine << here)
            leave = base + ((1 - mine) << here)
            keep[n] = source[stay, :, cols] + came[stay, :, cols].astype(F32)
            send[n] = (source[leave, :, cols] + came[leave, :, cols].astype(F32)).astype(BF)


def last_grads_kernel(held_a, held_b, moved_a, moved_b, qkv, proj):
    share = proj.shape[0]
    a = held_a[0] + moved_a[0].astype(F32)
    b = held_b[0] + moved_b[0].astype(F32)
    qkv[0] = a[:, :share].astype(BF)
    qkv[1] = a[:, share:].astype(BF)
    qkv[2] = b[:, :share].astype(BF)
    proj[...] = b[:, share:].T.astype(BF)


def finish_kernel(who, x_in, c_in, gain_in, keep, recv, stats, stats_in, *refs):
    tokens = keep.shape[1]
    full = x_in.shape[-1]
    own, swap = refs[-2:] if len(refs) == 2 else refs[3:5]
    x = x_in[...].reshape(tokens, full)
    standard, inverse = standardize(x)
    both = (stats[:, :tokens] + stats_in[:, :tokens]).T
    mean_plain, mean_cross = both[:, 0:1], both[:, 1:2]
    out = halves(x.astype(F32), who)[0] + keep[0] + recv[0].astype(F32)
    scaled = (keep[1] + recv[1].astype(F32)) * halves(gain_in[...].reshape(1, full), who)[0]
    through = inverse * (scaled - mean_plain - halves(standard, who)[0] * mean_cross)
    back = halves(c_in[...].reshape(tokens, full).astype(F32), who)[0] + through
    for i, value in enumerate((out, back)):
        a, b = own_and_other(value, who)
        own[i] = a.astype(BF)
        swap[i * tokens : (i + 1) * tokens] = b.astype(BF)
    if len(refs) > 2:
        gains_a, gains_b, stats_other = refs[:3]
        own_gain = refs[5]
        half = full // 2
        sent = stats_in[:1, tokens : tokens + half] + stats_other[:1, tokens : tokens + half]
        a, b = own_and_other(gains_a[...] + gains_b[...] + sent, who)
        own_gain[...] = a
        top, rest = two_parts(b)
        row = lax.broadcasted_iota(jnp.int32, (16, b.shape[1]), 0)
        swap[2 * tokens :] = jnp.where(row == 0, top, jnp.where(row == 1, rest, 0.0)).astype(BF)


def pack_kernel(frames, who, own_a, own_b, recv_a, recv_b, own_gain, out, held):
    tokens, share = own_a.shape[1:]
    chunk = tokens // frames
    j = who[0]
    top = recv_a[2 * tokens : 2 * tokens + 2].astype(F32)
    value = own_gain[...] + top[:1] + top[1:]
    lanes = out.shape[2]
    n_parts = -(-share // lanes)
    extra = out.shape[1] - 2 * share
    block = jnp.zeros((extra, lanes), F32)
    at = lax.broadcasted_iota(jnp.int32, (extra, lanes), 0)
    row = 0
    for part in two_parts(value):
        if n_parts * lanes > share:
            part = jnp.concatenate([part, jnp.zeros((1, n_parts * lanes - share), F32)], axis=1)
        for i in range(n_parts):
            block = jnp.where(at == row, part[:, i * lanes : (i + 1) * lanes], block)
            row += 1
    for i in range(2):
        for s in range(frames):
            rows = slice(s * chunk, (s + 1) * chunk)
            sent = slice(i * tokens + s * chunk, i * tokens + (s + 1) * chunk)
            held[i, s, j] = own_a[i, rows].astype(F32)
            held[i, s, j ^ 2] = own_b[i, rows].astype(F32)
            held[i, s, j ^ 1] = recv_a[sent].astype(F32)
            held[i, s, j ^ 3] = recv_b[sent].astype(F32)
            turned = held[i, s].reshape(4 * chunk, share).T.astype(BF)
            out[s, i * share : (i + 1) * share] = turned
    for s in range(frames):
        out[s, 2 * share :] = block.astype(BF)


def assemble_kernel(parts, first, second, total, held, sems):
    n_slots, rows, lanes = parts.shape
    share = first.shape[0]
    copies = []
    for i, out in enumerate((first, second)):
        for s in range(n_slots):
            copies.append(
                pltpu.make_async_copy(
                    parts.at[s, pl.ds(i * share, share)],
                    out.at[:, pl.ds(s * lanes, lanes)],
                    sems.at[i * n_slots + s],
                )
            )
    copies.append(
        pltpu.make_async_copy(
            parts.at[:, pl.ds(2 * share, rows - 2 * share)], held, sems.at[2 * n_slots]
        )
    )
    for copy in copies:
        copy.start()
    for copy in copies:
        copy.wait()
    value = held[0].astype(F32)
    for s in range(1, n_slots):
        value = value + held[s].astype(F32)
    n_parts = -(-share // lanes)
    value = value[:n_parts] + value[n_parts : 2 * n_parts]
    value = jnp.concatenate([value[i : i + 1] for i in range(n_parts)], axis=1)
    total[...] = value[:, :share]


def call(kernel, outs, *args, scalars=1, scratch=(), in_hbm=(), out_hbm=(), limit=None):
    def space(i, hbm):
        return pl.BlockSpec(memory_space=pl.ANY if i in hbm else pltpu.VMEM)

    return pl.pallas_call(
        kernel,
        out_shape=[jax.ShapeDtypeStruct(shape, kind) for shape, kind in outs],
        in_specs=[pl.BlockSpec(memory_space=pltpu.SMEM)] * scalars
        + [space(i, in_hbm) for i in range(scalars, len(args))],
        out_specs=[space(i, out_hbm) for i in range(len(outs))],
        scratch_shapes=scratch,
        compiler_params=pltpu.CompilerParams(vmem_limit_bytes=limit or VMEM_LIMIT),
    )(*args)


def block(frames_in, norm_gain, w_qkv, w_out, keep_runs, out_cotangent):
    _, place_total, width = frames_in.shape
    n_tm, n_te = lax.axis_size("tm"), lax.axis_size("tensor")
    frames = n_tm
    direct = n_tm <= 8
    n_near = n_tm // 2
    chunk = place_total // (n_tm * n_te)
    tokens = frames * chunk
    rows = 16 if chunk % 16 == 0 else chunk
    k = lax.axis_index("tm").astype(jnp.int32)
    j = lax.axis_index("tensor").astype(jnp.int32)
    where, who = k.reshape(1), j.reshape(1)
    share = w_qkv.shape[2]
    pair = 2 * share
    half = width // 2
    lanes = n_te * chunk

    gain = norm_gain

    def gather_chunks(value):
        mine = lax.dynamic_index_in_dim(
            value.reshape(n_tm, n_te, chunk, width), j, 1, keepdims=False
        )
        first = lax.all_to_all(mine, "tm", split_axis=0, concat_axis=0, tiled=True)
        return first, exchange(first, "tensor", 2)

    w_own = jnp.transpose(w_qkv, (1, 2, 0))
    w_other = exchange(w_own, "tensor", 1)
    out_other = exchange(w_out, "tensor", 1)
    if direct:
        (x_mine,) = call(
            send_x_kernel, [((n_tm, chunk, width), BF)],
            who, frames_in.reshape(n_tm, n_te, chunk, width),
            in_hbm=(1,), limit=WHOLE_VMEM,
            scratch=[pltpu.SemaphoreType.DMA((n_tm,))],
        )
        parts = call(
            functools.partial(send_c_kernel, n_near, n_tm),
            [((2, chunk, width), BF)] * n_near + [((chunk, width), BF)] * (n_tm - n_near),
            where, who, out_cotangent.reshape(n_tm, n_te, chunk, width),
            scalars=2, in_hbm=(2,), limit=WHOLE_VMEM,
            scratch=[pltpu.SemaphoreType.DMA((n_tm + n_near,))],
        )
        first = lax.all_to_all(x_mine, "tm", split_axis=0, concat_axis=0, tiled=True)
        xs = (first, exchange(first, "tensor", 2))
        far = [exchange(parts[s], "tm", s) for s in range(n_near, n_tm)]
        near = [parts[0]] + [exchange(parts[s], "tm", s) for s in range(1, n_near)]
        (stacked,) = call(
            stack_kernel, [((n_tm - n_near, chunk, width), BF)], *far,
            scalars=0,
        )
        passed = exchange(stacked, "tensor", 2)
        cs = (near + far, near + [passed] * (n_tm - n_near))
        picks = [
            [0] * n_near + [None] * (n_tm - n_near), [1] * n_near + list(range(n_tm - n_near))
        ]
    else:
        xs = gather_chunks(frames_in)
        cs = tuple([value] for value in gather_chunks(out_cotangent))
        picks = [[None], [None]]
    matrices = (w_own, w_other, w_out, out_other)

    runs = jnp.transpose(keep_runs, (0, 2, 1))
    cube = (frames, chunk)
    done, recvs, stats_in = [], [], []
    for g in range(2):
        done.append(
            call(
                functools.partial(attend_kernel, frames, rows, picks[g], n_te, g),
                [
                    (cube + (width,), BF),
                    ((tokens, width), BF),
                    (cube + (pair,), BF),
                    (cube + (3 * pair,), BF),
                    ((2, tokens, half), F32),
                    ((2, tokens, half), BF),
                    ((8, tokens + -(-half // LANES) * LANES), F32),
                    ((1, half), F32),
                ],
                who, where, gain, *matrices, runs, xs[g], *cs[g],
                scalars=2,
            )
        )
        recvs.append(exchange(done[g][5], "tensor", 2))
        stats_in.append(exchange(done[g][6], "tensor", 2))

    flat = lambda value: value.reshape(tokens, value.shape[-1])
    grad_keep, grad_send = call(
        grads_kernel,
        [((width, 4 * share), F32), ((width, 4 * share), BF)],
        done[0][1], done[1][1], flat(done[0][3]), flat(done[1][3]),
        flat(done[0][0]), flat(done[1][0]), flat(done[0][2]), flat(done[1][2]),
        scalars=0,
    )
    grad_recv = exchange(grad_send, "tensor", 1)
    per = width // n_tm
    bits = [1 << i for i in range(n_tm.bit_length() - 1)]
    column = 2 * share
    orders = (bits, bits[1::-1] + bits[2:])
    held = [grad_keep.reshape(n_tm, per, 4 * share)]
    moved = [grad_recv.reshape(n_tm, per, 4 * share)]
    for step in range(len(bits)):
        count = n_tm >> (step + 1)
        piece = (count, per, column)
        result = call(
            functools.partial(halve_kernel, n_tm, orders, step, len(held)),
            [(piece, F32), (piece, BF)] * 2,
            where, *held, *moved,
        )
        held = [result[0], result[2]]
        moved = [exchange(result[2 * i + 1], "tm", orders[i][step]) for i in range(2)]
    grad_qkv, grad_proj = call(
        last_grads_kernel,
        [((3, per, share), BF), ((share, per), BF)],
        *held, *moved,
        scalars=0,
    )
    grad_qkv = jnp.transpose(grad_qkv, (1, 0, 2))

    owns, swapped = [None, None], [None, None]
    for g in (1, 0):
        c_all, _, _, _, keep, _, stats, gains = done[g]
        outs = [((2, tokens, share), BF), ((2 * tokens + (0 if g else 16), share), BF)]
        more = ()
        if g == 0:
            outs.append(((1, share), F32))
            more = (gains, done[1][7], stats_in[0])
        result = call(
            finish_kernel, outs,
            who, xs[g], c_all, gain, keep, recvs[1 - g], stats, stats_in[1 - g], *more,
        )
        owns[g], swap = result[:2]
        swapped[g] = exchange(swap, "tensor", 1)
        if g == 0:
            own_gain = result[2]

    if direct:
        n_parts = -(-share // lanes)
        extra = -(-2 * n_parts // 16) * 16
        (message,) = call(
            functools.partial(pack_kernel, frames),
            [((frames, 2 * share + extra, lanes), BF)],
            who, *owns, *swapped, own_gain,
            scratch=[pltpu.VMEM((2, frames, n_te, chunk, share), F32)],
        )
        message = lax.all_to_all(message, "tm", split_axis=0, concat_axis=0, tiled=True)
        whole = ((share, place_total), BF)
        block_out, grad_in, total = call(
            assemble_kernel, [whole, whole, ((1, share), F32)], message,
            scalars=0, in_hbm=(0,), out_hbm=(0, 1),
            scratch=[
                pltpu.VMEM((n_tm, extra, lanes), BF),
                pltpu.SemaphoreType.DMA((2 * n_tm + 1,)),
            ],
        )
        block_out, grad_in = block_out.T, grad_in.T
        grad_gain = total.reshape(share)
    else:
        order = jnp.arange(n_te, dtype=jnp.int32) ^ j
        four = jnp.stack(
            [owns[0], swapped[0][: 2 * tokens].reshape(2, tokens, share),
             owns[1], swapped[1].reshape(2, tokens, share)]
        )[order].reshape(n_te, 2, frames, chunk, share)
        message = jnp.transpose(four, (2, 1, 0, 3, 4)).reshape(frames, 2, lanes, share)
        message = lax.all_to_all(message, "tm", split_axis=0, concat_axis=0, tiled=True)
        block_out = message[:, 0].reshape(place_total, share)
        grad_in = message[:, 1].reshape(place_total, share)
        sent = swapped[0][2 * tokens : 2 * tokens + 2].astype(F32)
        grad_gain = lax.psum(own_gain[0] + sent[0] + sent[1], "tm")
    return (block_out[None], grad_in[None], grad_qkv, grad_proj, grad_gain)


def solution(mesh):
    in_specs = (
        P("tm", None, None),
        P(),
        P(None, None, "tensor"),
        P("tensor", None),
        P(),
        P("tm", None, None),
    )
    out_specs = (
        P("tm", None, "tensor"),
        P("tm", None, "tensor"),
        P("tm", None, "tensor"),
        P("tensor", "tm"),
        P("tensor"),
    )
    return jax.shard_map(block, mesh=mesh, in_specs=in_specs, out_specs=out_specs, check_vma=False)
```

```python
import functools

import jax
import jax.numpy as jnp
from jax import lax
from jax.experimental import pallas as pl
from jax.experimental.pallas import tpu as pltpu
from jax.sharding import PartitionSpec as P

D = 768
H = 12
HEAD = D // H
LANES = 128
EPS = 1e-05
MASKED = -1000000000.0

BF = jnp.bfloat16
F32 = jnp.float32
VMEM_LIMIT = 12 * 1024 * 1024
WHOLE_VMEM = 61*1024*1024


def exchange(value, axis, bit):
    size = lax.axis_size(axis)
    return lax.ppermute(value, axis, [(i, i ^ bit) for i in range(size)])


def dot(a, b):
    return lax.dot_general(a, b, (((1,), (0,)), ((), ())), preferred_element_type=F32)


def dot_t(a, b):
    return lax.dot_general(a, b, (((1,), (1,)), ((), ())), preferred_element_type=F32)


def t_dot(a, b):
    return lax.dot_general(a, b, (((0,), (0,)), ((), ())), preferred_element_type=F32)


def standardize(x):
    x = x.astype(F32)
    shifted = x - jnp.mean(x, axis=-1, keepdims=True)
    inverse = lax.rsqrt(jnp.mean(shifted * shifted, axis=-1, keepdims=True) + EPS)
    return shifted * inverse, inverse


def block_rows(value, frames, b, rows):
    q = value.shape[0] // frames
    if q == rows:
        return value
    cut = value.reshape(frames, q, value.shape[1])[:, b * rows : (b + 1) * rows]
    return cut.reshape(frames * rows, value.shape[1])


def split_heads(value):
    lane = lax.broadcasted_iota(jnp.int32, value.shape, 1)
    zero = jnp.zeros_like(value)
    return jnp.concatenate(
        [jnp.where(lane < HEAD, value, zero), jnp.where(lane >= HEAD, value, zero)], axis=0
    )


def join_heads(value):
    n = value.shape[0] // 2
    lane = lax.broadcasted_iota(jnp.int32, (n, value.shape[1]), 1)
    return jnp.where(lane < HEAD, value[:n], value[n:])


def put_rows(ref, b, rows, col, value):
    ref[:, b * rows : (b + 1) * rows, col : col + value.shape[1]] = value.reshape(
        ref.shape[0], rows, value.shape[1]
    )


def all_rows(parts):
    return jnp.concatenate(list(parts), axis=0)


def halves(value, who):
    half = value.shape[-1] // 2
    low, high = value[..., :half], value[..., half:]
    first = who[0] // 2 == 0
    return jnp.where(first, low, high), jnp.where(first, high, low)


def own_and_other(value, who):
    share = value.shape[-1] // 2
    low, high = value[..., :share], value[..., share:]
    first = who[0] % 2 == 0
    return jnp.where(first, low, high), jnp.where(first, high, low)


def two_parts(value):
    top = value.astype(BF).astype(F32)
    return top, value - top


def copy_all(pairs, sems):
    copies = [pltpu.make_async_copy(src, dst, sems.at[i]) for i, (src, dst) in enumerate(pairs)]
    for copy in copies:
        copy.start()
    for copy in copies:
        copy.wait()


def send_x_kernel(j, x_in, x_out, sems):
    copy_all([(x_in.at[i, j[0]], x_out.at[i]) for i in range(x_out.shape[0])], sems)


def send_c_kernel(n_near, n_slots, k, j, c_in, *refs):
    outs, sems = refs[:n_slots], refs[n_slots]
    pairs = []
    for s in range(n_slots):
        if s < n_near:
            for g in range(2):
                pairs.append((c_in.at[k[0] ^ s, j[0] ^ (2 * g)], outs[s].at[g]))
        else:
            pairs.append((c_in.at[k[0] ^ s, j[0]], outs[s]))
    copy_all(pairs, sems)


def stack_kernel(*refs):
    parts, out = refs[:-1], refs[-1]
    for i, ref in enumerate(parts):
        out[i] = ref[...]


def kept_row(runs, frames, rows, first):
    lane = lax.broadcasted_iota(jnp.int32, (frames, frames * rows), 1)
    frame = lax.broadcasted_iota(jnp.int32, (frames, frames * rows), 0)
    place = first + lane % rows
    begins, lengths = runs[:, 0, :], runs[:, 1, :]
    hits = jnp.zeros((frames, frames * rows), F32)
    for r in range(begins.shape[1]):
        begin = begins[:, r : r + 1]
        here = (place >= begin) & (place < begin + lengths[:, r : r + 1])
        hits = jnp.where(here, 1.0, hits)
    return jnp.sum(jnp.where(frame == lane // rows, hits, 0.0), axis=0, keepdims=True)


def attend_kernel(
    frames, rows, picks, n_te, g, who, where, gain_in, wa, wb, oa, ob, runs, x_in, *refs
):
    c_in, rest = refs[: len(picks)], refs[len(picks) :]
    c_all, normed, mixed, pcot, keep, send, stats, gains = rest
    if len(picks) == 1:
        c_all[...] = c_in[0][...]
    else:
        for s, (ref, pick) in enumerate(zip(c_in, picks)):
            c_all[where[0] ^ s] = ref[...] if pick is None else ref[pick]
    gain = gain_in[...].reshape(1, x_in.shape[2])
    wq, wk, wv = (all_rows((wa[i], wb[i])) for i in range(3))
    wout = all_rows((oa[...], ob[...]))
    width, full = wout.shape
    chunk = x_in.shape[1]
    tokens = frames * chunk
    n_rows = frames * rows
    standard, _ = standardize(x_in[...].reshape(tokens, full))
    n = (standard * gain).astype(BF)
    normed[...] = n
    qs, ks, vs = (dot_t(n, w).astype(BF) for w in (wq, wk, wv))
    c = c_all[...].reshape(tokens, full)
    mc = dot_t(c, wout).astype(BF)
    row = lax.broadcasted_iota(jnp.int32, (n_rows, n_rows), 0)
    col = lax.broadcasted_iota(jnp.int32, (n_rows, n_rows), 1)
    first = (where[0] * n_te + (who[0] ^ (2 * g))) * chunk
    for b in range(chunk // rows):
        across = kept_row(runs, frames, rows, first + b * rows)
        down = jnp.sum(jnp.where(row == col, across, 0.0), axis=1, keepdims=True)
        inside = jnp.where(row % rows == col % rows, across * down, 0.0)
        for p in range(width // LANES):
            cols = slice(p * LANES, (p + 1) * LANES)
            q, k, v, dm = (block_rows(z[:, cols], frames, b, rows) for z in (qs, ks, vs, mc))
            kk, vv = split_heads(k), split_heads(v)
            s = dot_t(q, kk) * HEAD ** (-0.5)
            dw = dot_t(dm, vv).astype(BF).astype(F32)
            w_parts, d_parts = [], []
            for e in range(2):
                part = jnp.where(inside > 0, s[:, e * n_rows : (e + 1) * n_rows], MASKED)
                top = jnp.max(part, axis=-1, keepdims=True)
                ex = jnp.exp(part - top) * inside
                total = jnp.sum(ex, axis=-1, keepdims=True)
                we = ex / jnp.where(total > 0, total, 1.0)
                de = dw[:, e * n_rows : (e + 1) * n_rows]
                inner = jnp.sum(we * de, axis=-1, keepdims=True)
                w_parts.append(we.astype(BF))
                d_parts.append((we * (de - inner) * HEAD ** (-0.5)).astype(BF))
            w = jnp.concatenate(w_parts, axis=1)
            ds = jnp.concatenate(d_parts, axis=1)
            put_rows(mixed, b, rows, p * LANES, dot(w, vv).astype(BF))
            put_rows(pcot, b, rows, p * LANES, dot(ds, kk).astype(BF))
            put_rows(pcot, b, rows, width + p * LANES, join_heads(t_dot(ds, q)).astype(BF))
            put_rows(pcot, b, rows, 2 * width + p * LANES, join_heads(t_dot(w, dm)).astype(BF))
    y = dot(mixed[...].reshape(tokens, width), wout)
    mine, other = halves(y, who)
    keep[0] = mine
    send[0] = other.astype(BF)
    pc = pcot[...].reshape(tokens, 3 * width)
    nc = dot(pc, all_rows((wq, wk, wv)))
    nn = n.astype(F32) * nc
    mean_plain = jnp.sum(nc * gain, axis=-1, keepdims=True)
    mean_cross = jnp.sum(nn, axis=-1, keepdims=True)
    total_gain = jnp.sum(nn, axis=0, keepdims=True) / gain
    lane = lax.broadcasted_iota(jnp.int32, (tokens, LANES), 1)
    both = jnp.where(lane == 0, mean_plain, mean_cross) * (1.0 / full)
    half = full // 2
    stats[:, :tokens] = both.T[:8]
    mine, other = halves(nc, who)
    keep[1] = mine
    send[1] = other.astype(BF)
    mine, other = halves(total_gain, who)
    gains[...] = mine
    stats[:1, tokens : tokens + half] = other


def grads_kernel(n0, n1, p0, p1, c0, c1, m0, m1, keep, send):
    width = m0.shape[1]
    share = width // 2
    columns = []
    for which in range(3):
        cols = slice(which * width, (which + 1) * width)
        columns.append(t_dot(n0[...], p0[:, cols]) + t_dot(n1[...], p1[:, cols]))
    columns.append(t_dot(c0[...], m0[...]) + t_dot(c1[...], m1[...]))
    keep[...] = jnp.concatenate([v[:, :share] for v in columns], axis=1)
    send[...] = jnp.concatenate([v[:, share:] for v in columns], axis=1).astype(BF)


def halve_kernel(n_blocks, orders, step, n_held, where, *refs):
    held, moved, outs = refs[:n_held], refs[n_held : 2 * n_held], refs[2 * n_held :]
    k = where[0]
    for i, order in enumerate(orders):
        column = outs[2 * i].shape[-1]
        cols = slice(i * column, (i + 1) * column) if n_held == 1 else slice(None)
        keep, send = outs[2 * i : 2 * i + 2]
        source, came = held[i % n_held], moved[i % n_held]
        left = [bit for bit in (1 << b for b in range(n_blocks.bit_length())) if bit < n_blocks]
        left = [bit for bit in left if bit not in order[:step]]
        here = left.index(order[step])
        mine = (k // order[step]) % 2
        for n in range(keep.shape[0]):
            low = n % (1 << here)
            base = ((n >> here) << (here + 1)) + low
            stay = base + (mine << here)
            leave = base + ((1 - mine) << here)
            keep[n] = source[stay, :, cols] + came[stay, :, cols].astype(F32)
            send[n] = (source[leave, :, cols] + came[leave, :, cols].astype(F32)).astype(BF)


def last_grads_kernel(held_a, held_b, moved_a, moved_b, qkv, proj):
    share = proj.shape[0]
    a = held_a[0] + moved_a[0].astype(F32)
    b = held_b[0] + moved_b[0].astype(F32)
    qkv[0] = a[:, :share].astype(BF)
    qkv[1] = a[:, share:].astype(BF)
    qkv[2] = b[:, :share].astype(BF)
    proj[...] = b[:, share:].T.astype(BF)


def finish_kernel(who, x_in, c_in, gain_in, keep, recv, stats, stats_in, *refs):
    tokens = keep.shape[1]
    full = x_in.shape[-1]
    own, swap = refs[-2:] if len(refs) == 2 else refs[3:5]
    x = x_in[...].reshape(tokens, full)
    standard, inverse = standardize(x)
    both = (stats[:, :tokens] + stats_in[:, :tokens]).T
    mean_plain, mean_cross = both[:, 0:1], both[:, 1:2]
    out = halves(x.astype(F32), who)[0] + keep[0] + recv[0].astype(F32)
    scaled = (keep[1] + recv[1].astype(F32)) * halves(gain_in[...].reshape(1, full), who)[0]
    through = inverse * (scaled - mean_plain - halves(standard, who)[0] * mean_cross)
    back = halves(c_in[...].reshape(tokens, full).astype(F32), who)[0] + through
    for i, value in enumerate((out, back)):
        a, b = own_and_other(value, who)
        own[i] = a.astype(BF)
        swap[i * tokens : (i + 1) * tokens] = b.astype(BF)
    if len(refs) > 2:
        gains_a, gains_b, stats_other = refs[:3]
        own_gain = refs[5]
        half = full // 2
        sent = stats_in[:1, tokens : tokens + half] + stats_other[:1, tokens : tokens + half]
        a, b = own_and_other(gains_a[...] + gains_b[...] + sent, who)
        own_gain[...] = a
        top, rest = two_parts(b)
        row = lax.broadcasted_iota(jnp.int32, (16, b.shape[1]), 0)
        swap[2 * tokens :] = jnp.where(row == 0, top, jnp.where(row == 1, rest, 0.0)).astype(BF)


def pack_kernel(frames, who, where, own_a, own_b, recv_a, recv_b, own_gain, *refs):
    outs, held = refs[:frames], refs[frames]
    tokens, share = own_a.shape[1:]
    chunk = tokens // frames
    lanes = outs[0].shape[1]
    j = who[0]
    top = recv_a[2 * tokens : 2 * tokens + 2].astype(F32)
    value = own_gain[...] + top[:1] + top[1:]
    n_parts = -(-share // lanes)
    extra = outs[0].shape[0] - 2 * share
    block = jnp.zeros((extra, lanes), F32)
    at = lax.broadcasted_iota(jnp.int32, (extra, lanes), 0)
    row = 0
    for part in two_parts(value):
        if n_parts * lanes > share:
            part = jnp.concatenate([part, jnp.zeros((1, n_parts * lanes - share), F32)], axis=1)
        for i in range(n_parts):
            block = jnp.where(at == row, part[:, i * lanes : (i + 1) * lanes], block)
            row += 1
    for s in range(frames):
        frame = where[0] ^ s
        rows = pl.ds(pl.multiple_of(frame * chunk, chunk), chunk)
        for i in range(2):
            sent = pl.ds(pl.multiple_of(i * tokens + frame * chunk, chunk), chunk)
            held[i, s, j] = own_a[i, rows].astype(F32)
            held[i, s, j ^ 2] = own_b[i, rows].astype(F32)
            held[i, s, j ^ 1] = recv_a[sent].astype(F32)
            held[i, s, j ^ 3] = recv_b[sent].astype(F32)
            turned = held[i, s].reshape(4 * chunk, share).T.astype(BF)
            outs[s][i * share : (i + 1) * share] = turned
        outs[s][2 * share :] = block.astype(BF)


def assemble_kernel(n_slots, where, *refs):
    parts = refs[:n_slots]
    first, second, total, sems = refs[n_slots:]
    _, lanes = parts[0].shape
    share = first.shape[0]
    pairs = []
    for s, part in enumerate(parts):
        at = pl.ds(pl.multiple_of((where[0] ^ s) * lanes, lanes), lanes)
        for i, out in enumerate((first, second)):
            pairs.append((part.at[pl.ds(i * share, share)], out.at[:, at]))
    copies = [pltpu.make_async_copy(src, dst, sems.at[i]) for i, (src, dst) in enumerate(pairs)]
    for copy in copies:
        copy.start()
    value = parts[0][2 * share :].astype(F32)
    for part in parts[1:]:
        value = value + part[2 * share :].astype(F32)
    n_parts = -(-share // lanes)
    value = value[:n_parts] + value[n_parts : 2 * n_parts]
    value = jnp.concatenate([value[i : i + 1] for i in range(n_parts)], axis=1)
    total[...] = value[:, :share]
    for copy in copies:
        copy.wait()


def call(kernel, outs, *args, scalars=1, scratch=(), in_hbm=(), out_hbm=(), limit=None):
    def space(i, hbm):
        return pl.BlockSpec(memory_space=pl.ANY if i in hbm else pltpu.VMEM)

    return pl.pallas_call(
        kernel,
        out_shape=[jax.ShapeDtypeStruct(shape, kind) for shape, kind in outs],
        in_specs=[pl.BlockSpec(memory_space=pltpu.SMEM)] * scalars
        + [space(i, in_hbm) for i in range(scalars, len(args))],
        out_specs=[space(i, out_hbm) for i in range(len(outs))],
        scratch_shapes=scratch,
        compiler_params=pltpu.CompilerParams(vmem_limit_bytes=limit or VMEM_LIMIT),
    )(*args)


def block(frames_in, norm_gain, w_qkv, w_out, keep_runs, out_cotangent):
    _, place_total, width = frames_in.shape
    n_tm, n_te = lax.axis_size("tm"), lax.axis_size("tensor")
    frames = n_tm
    direct = n_tm <= 8
    n_near = n_tm // 2
    chunk = place_total // (n_tm * n_te)
    tokens = frames * chunk
    rows = 16 if chunk % 16 == 0 else chunk
    k = lax.axis_index("tm").astype(jnp.int32)
    j = lax.axis_index("tensor").astype(jnp.int32)
    where, who = k.reshape(1), j.reshape(1)
    share = w_qkv.shape[2]
    pair = 2 * share
    half = width // 2
    lanes = n_te * chunk

    gain = norm_gain

    def gather_chunks(value):
        mine = lax.dynamic_index_in_dim(
            value.reshape(n_tm, n_te, chunk, width), j, 1, keepdims=False
        )
        first = lax.all_to_all(mine, "tm", split_axis=0, concat_axis=0, tiled=True)
        return first, exchange(first, "tensor", 2)

    w_own = jnp.transpose(w_qkv, (1, 2, 0))
    w_other = exchange(w_own, "tensor", 1)
    out_other = exchange(w_out, "tensor", 1)
    if direct:
        (x_mine,) = call(
            send_x_kernel, [((n_tm, chunk, width), BF)],
            who, frames_in.reshape(n_tm, n_te, chunk, width),
            in_hbm=(1,), limit=WHOLE_VMEM,
            scratch=[pltpu.SemaphoreType.DMA((n_tm,))],
        )
        parts = call(
            functools.partial(send_c_kernel, n_near, n_tm),
            [((2, chunk, width), BF)] * n_near + [((chunk, width), BF)] * (n_tm - n_near),
            where, who, out_cotangent.reshape(n_tm, n_te, chunk, width),
            scalars=2, in_hbm=(2,), limit=WHOLE_VMEM,
            scratch=[pltpu.SemaphoreType.DMA((n_tm + n_near,))],
        )
        first = lax.all_to_all(x_mine, "tm", split_axis=0, concat_axis=0, tiled=True)
        xs = (first, exchange(first, "tensor", 2))
        far = [exchange(parts[s], "tm", s) for s in range(n_near, n_tm)]
        near = [parts[0]] + [exchange(parts[s], "tm", s) for s in range(1, n_near)]
        (stacked,) = call(
            stack_kernel, [((n_tm - n_near, chunk, width), BF)], *far,
            scalars=0,
        )
        passed = exchange(stacked, "tensor", 2)
        cs = (near + far, near + [passed] * (n_tm - n_near))
        picks = [
            [0] * n_near + [None] * (n_tm - n_near), [1] * n_near + list(range(n_tm - n_near))
        ]
    else:
        xs = gather_chunks(frames_in)
        cs = tuple([value] for value in gather_chunks(out_cotangent))
        picks = [[None], [None]]
    matrices = (w_own, w_other, w_out, out_other)

    runs = jnp.transpose(keep_runs, (0, 2, 1))
    cube = (frames, chunk)
    done, recvs, stats_in = [], [], []
    for g in range(2):
        done.append(
            call(
                functools.partial(attend_kernel, frames, rows, picks[g], n_te, g),
                [
                    (cube + (width,), BF),
                    ((tokens, width), BF),
                    (cube + (pair,), BF),
                    (cube + (3 * pair,), BF),
                    ((2, tokens, half), F32),
                    ((2, tokens, half), BF),
                    ((8, tokens + -(-half // LANES) * LANES), F32),
                    ((1, half), F32),
                ],
                who, where, gain, *matrices, runs, xs[g], *cs[g],
                scalars=2,
            )
        )
        recvs.append(exchange(done[g][5], "tensor", 2))
        stats_in.append(exchange(done[g][6], "tensor", 2))

    flat = lambda value: value.reshape(tokens, value.shape[-1])
    grad_keep, grad_send = call(
        grads_kernel,
        [((width, 4 * share), F32), ((width, 4 * share), BF)],
        done[0][1], done[1][1], flat(done[0][3]), flat(done[1][3]),
        flat(done[0][0]), flat(done[1][0]), flat(done[0][2]), flat(done[1][2]),
        scalars=0,
    )
    grad_recv = exchange(grad_send, "tensor", 1)
    per = width // n_tm
    bits = [1 << i for i in range(n_tm.bit_length() - 1)]
    column = 2 * share
    orders = (bits, bits[1::-1] + bits[2:])
    held = [grad_keep.reshape(n_tm, per, 4 * share)]
    moved = [grad_recv.reshape(n_tm, per, 4 * share)]
    for step in range(len(bits)):
        count = n_tm >> (step + 1)
        piece = (count, per, column)
        result = call(
            functools.partial(halve_kernel, n_tm, orders, step, len(held)),
            [(piece, F32), (piece, BF)] * 2,
            where, *held, *moved,
        )
        held = [result[0], result[2]]
        moved = [exchange(result[2 * i + 1], "tm", orders[i][step]) for i in range(2)]
    grad_qkv, grad_proj = call(
        last_grads_kernel,
        [((3, per, share), BF), ((share, per), BF)],
        *held, *moved,
        scalars=0,
    )
    grad_qkv = jnp.transpose(grad_qkv, (1, 0, 2))

    owns, swapped = [None, None], [None, None]
    for g in (1, 0):
        c_all, _, _, _, keep, _, stats, gains = done[g]
        outs = [((2, tokens, share), BF), ((2 * tokens + (0 if g else 16), share), BF)]
        more = ()
        if g == 0:
            outs.append(((1, share), F32))
            more = (gains, done[1][7], stats_in[0])
        result = call(
            finish_kernel, outs,
            who, xs[g], c_all, gain, keep, recvs[1 - g], stats, stats_in[1 - g], *more,
        )
        owns[g], swap = result[:2]
        swapped[g] = exchange(swap, "tensor", 1)
        if g == 0:
            own_gain = result[2]

    if direct:
        n_parts = -(-share // lanes)
        extra = -(-2 * n_parts // 16) * 16
        messages = call(
            functools.partial(pack_kernel, frames),
            [((2 * share + extra, lanes), BF)] * frames,
            who, where, *owns, *swapped, own_gain,
            scalars=2,
            scratch=[pltpu.VMEM((2, frames, n_te, chunk, share), F32)],
        )
        messages = [messages[0]] + [exchange(messages[s], "tm", s) for s in range(1, n_tm)]
        whole = ((share, place_total), BF)
        block_out, grad_in, total = call(
            functools.partial(assemble_kernel, n_tm),
            [whole, whole, ((1, share), F32)], where, *messages,
            out_hbm=(0, 1), scratch=[pltpu.SemaphoreType.DMA((2 * n_tm,))],
        )
        block_out, grad_in = block_out.T, grad_in.T
        grad_gain = total.reshape(share)
    else:
        order = jnp.arange(n_te, dtype=jnp.int32) ^ j
        four = jnp.stack(
            [owns[0], swapped[0][: 2 * tokens].reshape(2, tokens, share),
             owns[1], swapped[1].reshape(2, tokens, share)]
        )[order].reshape(n_te, 2, frames, chunk, share)
        message = jnp.transpose(four, (2, 1, 0, 3, 4)).reshape(frames, 2, lanes, share)
        message = lax.all_to_all(message, "tm", split_axis=0, concat_axis=0, tiled=True)
        block_out = message[:, 0].reshape(place_total, share)
        grad_in = message[:, 1].reshape(place_total, share)
        sent = swapped[0][2 * tokens : 2 * tokens + 2].astype(F32)
        grad_gain = lax.psum(own_gain[0] + sent[0] + sent[1], "tm")
    return (block_out[None], grad_in[None], grad_qkv, grad_proj, grad_gain)


def solution(mesh):
    in_specs = (
        P("tm", None, None),
        P(),
        P(None, None, "tensor"),
        P("tensor", None),
        P(),
        P("tm", None, None),
    )
    out_specs = (
        P("tm", None, "tensor"),
        P("tm", None, "tensor"),
        P("tm", None, "tensor"),
        P("tensor", "tm"),
        P("tensor"),
    )
    return jax.shard_map(block, mesh=mesh, in_specs=in_specs, out_specs=out_specs, check_vma=False)
```

```python
import functools

import jax
import jax.numpy as jnp
from jax import lax
from jax.experimental import pallas as pl
from jax.experimental.pallas import tpu as pltpu
from jax.sharding import PartitionSpec as P

D = 768
H = 12
HEAD = D // H
LANES = 128
EPS = 1e-05
MASKED = -1000000000.0

BF = jnp.bfloat16
F32 = jnp.float32
VMEM_LIMIT = 12 * 1024 * 1024
WHOLE_VMEM = 61*1024*1024


def exchange(value, axis, bit):
    size = lax.axis_size(axis)
    return lax.ppermute(value, axis, [(i, i ^ bit) for i in range(size)])


def dot(a, b):
    return lax.dot_general(a, b, (((1,), (0,)), ((), ())), preferred_element_type=F32)


def dot_t(a, b):
    return lax.dot_general(a, b, (((1,), (1,)), ((), ())), preferred_element_type=F32)


def t_dot(a, b):
    return lax.dot_general(a, b, (((0,), (0,)), ((), ())), preferred_element_type=F32)


def standardize(x):
    x = x.astype(F32)
    shifted = x - jnp.mean(x, axis=-1, keepdims=True)
    inverse = lax.rsqrt(jnp.mean(shifted * shifted, axis=-1, keepdims=True) + EPS)
    return shifted * inverse, inverse


def block_rows(value, frames, b, rows):
    q = value.shape[0] // frames
    if q == rows:
        return value
    cut = value.reshape(frames, q, value.shape[1])[:, b * rows : (b + 1) * rows]
    return cut.reshape(frames * rows, value.shape[1])


def split_heads(value):
    lane = lax.broadcasted_iota(jnp.int32, value.shape, 1)
    zero = jnp.zeros_like(value)
    return jnp.concatenate(
        [jnp.where(lane < HEAD, value, zero), jnp.where(lane >= HEAD, value, zero)], axis=0
    )


def join_heads(value):
    n = value.shape[0] // 2
    lane = lax.broadcasted_iota(jnp.int32, (n, value.shape[1]), 1)
    return jnp.where(lane < HEAD, value[:n], value[n:])


def put_rows(ref, b, rows, col, value):
    ref[:, b * rows : (b + 1) * rows, col : col + value.shape[1]] = value.reshape(
        ref.shape[0], rows, value.shape[1]
    )


def all_rows(parts):
    return jnp.concatenate(list(parts), axis=0)


def halves(value, who):
    half = value.shape[-1] // 2
    low, high = value[..., :half], value[..., half:]
    first = who[0] // 2 == 0
    return jnp.where(first, low, high), jnp.where(first, high, low)


def own_and_other(value, who):
    share = value.shape[-1] // 2
    low, high = value[..., :share], value[..., share:]
    first = who[0] % 2 == 0
    return jnp.where(first, low, high), jnp.where(first, high, low)


def two_parts(value):
    top = value.astype(BF).astype(F32)
    return top, value - top


def copy_all(pairs, sems):
    copies = [pltpu.make_async_copy(src, dst, sems.at[i]) for i, (src, dst) in enumerate(pairs)]
    for copy in copies:
        copy.start()
    for copy in copies:
        copy.wait()


def send_x_kernel(j, x_in, x_out, sems):
    copy_all([(x_in.at[i, j[0]], x_out.at[i]) for i in range(x_out.shape[0])], sems)


def send_c_kernel(n_near, n_slots, k, j, c_in, *refs):
    outs, sems = refs[:n_slots], refs[n_slots]
    pairs = []
    for s in range(n_slots):
        if s < n_near:
            for g in range(2):
                pairs.append((c_in.at[k[0] ^ s, j[0] ^ (2 * g)], outs[s].at[g]))
        else:
            pairs.append((c_in.at[k[0] ^ s, j[0]], outs[s]))
    copy_all(pairs, sems)


def stack_kernel(*refs):
    parts, out = refs[:-1], refs[-1]
    for i, ref in enumerate(parts):
        out[i] = ref[...]


def kept_row(runs, frames, rows, first):
    lane = lax.broadcasted_iota(jnp.int32, (frames, frames * rows), 1)
    frame = lax.broadcasted_iota(jnp.int32, (frames, frames * rows), 0)
    place = first + lane % rows
    begins, lengths = runs[:, 0, :], runs[:, 1, :]
    hits = jnp.zeros((frames, frames * rows), F32)
    for r in range(begins.shape[1]):
        begin = begins[:, r : r + 1]
        here = (place >= begin) & (place < begin + lengths[:, r : r + 1])
        hits = jnp.where(here, 1.0, hits)
    return jnp.sum(jnp.where(frame == lane // rows, hits, 0.0), axis=0, keepdims=True)


def attend_kernel(
    frames, rows, picks, n_te, g, who, where, gain_in, wa, wb, oa, ob, runs, x_in, *refs
):
    c_in, rest = refs[: len(picks)], refs[len(picks) :]
    c_all, normed, mixed, pcot, keep, send, stats, gains = rest
    if len(picks) == 1:
        c_all[...] = c_in[0][...]
    else:
        for s, (ref, pick) in enumerate(zip(c_in, picks)):
            c_all[where[0] ^ s] = ref[...] if pick is None else ref[pick]
    gain = gain_in[...].reshape(1, x_in.shape[2])
    wq, wk, wv = (all_rows((wa[i], wb[i])) for i in range(3))
    wout = all_rows((oa[...], ob[...]))
    width, full = wout.shape
    chunk = x_in.shape[1]
    tokens = frames * chunk
    n_rows = frames * rows
    standard, _ = standardize(x_in[...].reshape(tokens, full))
    n = (standard * gain).astype(BF)
    normed[...] = n
    qs, ks, vs = (dot_t(n, w).astype(BF) for w in (wq, wk, wv))
    c = c_all[...].reshape(tokens, full)
    mc = dot_t(c, wout).astype(BF)
    row = lax.broadcasted_iota(jnp.int32, (n_rows, n_rows), 0)
    col = lax.broadcasted_iota(jnp.int32, (n_rows, n_rows), 1)
    first = (where[0] * n_te + (who[0] ^ (2 * g))) * chunk
    for b in range(chunk // rows):
        across = kept_row(runs, frames, rows, first + b * rows)
        down = jnp.sum(jnp.where(row == col, across, 0.0), axis=1, keepdims=True)
        inside = jnp.where(row % rows == col % rows, across * down, 0.0)
        for p in range(width // LANES):
            cols = slice(p * LANES, (p + 1) * LANES)
            q, k, v, dm = (block_rows(z[:, cols], frames, b, rows) for z in (qs, ks, vs, mc))
            kk, vv = split_heads(k), split_heads(v)
            s = dot_t(q, kk) * HEAD ** (-0.5)
            dw = dot_t(dm, vv).astype(BF).astype(F32)
            w_parts, d_parts = [], []
            for e in range(2):
                part = jnp.where(inside > 0, s[:, e * n_rows : (e + 1) * n_rows], MASKED)
                top = jnp.max(part, axis=-1, keepdims=True)
                ex = jnp.exp(part - top) * inside
                total = jnp.sum(ex, axis=-1, keepdims=True)
                we = ex / jnp.where(total > 0, total, 1.0)
                de = dw[:, e * n_rows : (e + 1) * n_rows]
                inner = jnp.sum(we * de, axis=-1, keepdims=True)
                w_parts.append(we.astype(BF))
                d_parts.append((we * (de - inner) * HEAD ** (-0.5)).astype(BF))
            w = jnp.concatenate(w_parts, axis=1)
            ds = jnp.concatenate(d_parts, axis=1)
            put_rows(mixed, b, rows, p * LANES, dot(w, vv).astype(BF))
            put_rows(pcot, b, rows, p * LANES, dot(ds, kk).astype(BF))
            put_rows(pcot, b, rows, width + p * LANES, join_heads(t_dot(ds, q)).astype(BF))
            put_rows(pcot, b, rows, 2 * width + p * LANES, join_heads(t_dot(w, dm)).astype(BF))
    y = dot(mixed[...].reshape(tokens, width), wout)
    mine, other = halves(y, who)
    keep[0] = mine
    send[:tokens] = other.astype(BF)
    pc = pcot[...].reshape(tokens, 3 * width)
    nc = dot(pc, all_rows((wq, wk, wv)))
    nn = n.astype(F32) * nc
    mean_plain = jnp.sum(nc * gain, axis=-1, keepdims=True)
    mean_cross = jnp.sum(nn, axis=-1, keepdims=True)
    total_gain = jnp.sum(nn, axis=0, keepdims=True) / gain
    lane = lax.broadcasted_iota(jnp.int32, (tokens, LANES), 1)
    both = (jnp.where(lane == 0, mean_plain, mean_cross) * (1.0 / full)).T[:2]
    half = full // 2
    stats[...] = both
    mine, other = halves(nc, who)
    keep[1] = mine
    send[tokens : 2 * tokens] = other.astype(BF)
    mine, other = halves(total_gain, who)
    gains[...] = mine
    if half > tokens:
        both = jnp.concatenate([both, jnp.zeros((2, half - tokens), F32)], axis=1)
    sent = []
    for value in (both[:1], both[1:], other):
        sent += two_parts(value)
    send[2 * tokens :] = stacked_rows(sent, 16, half).astype(BF)


def stacked_rows(values, count, lanes):
    at = lax.broadcasted_iota(jnp.int32, (count, lanes), 0)
    block = jnp.zeros((count, lanes), F32)
    for i, value in enumerate(values):
        block = jnp.where(at == i, value, block)
    return block


def local_kernel(source, out):
    out[...] = source[...]


def grads_kernel(own, n0, n1, p0, p1, c0, c1, m0, m1, out):
    width = m0.shape[1]
    share = width // 2
    columns = []
    for which in range(4):
        if which < 3:
            left, right, base = (n0, n1), (p0, p1), which * width
        else:
            left, right, base = (c0, c1), (m0, m1), 0
        cols = slice(base, base + width)
        value = t_dot(left[0][...], right[0][:, cols]) + t_dot(left[1][...], right[1][:, cols])
        columns.append(value[:, :share] if own else value[:, share:])
    out[...] = jnp.concatenate(columns, axis=1).astype(out.dtype)


def halve_kernel(n_blocks, orders, step, n_held, where, *refs):
    held, moved, outs = refs[:n_held], refs[n_held : 2 * n_held], refs[2 * n_held :]
    k = where[0]
    for i, order in enumerate(orders):
        column = outs[2 * i].shape[-1]
        cols = slice(i * column, (i + 1) * column) if n_held == 1 else slice(None)
        keep, send = outs[2 * i : 2 * i + 2]
        source, came = held[i % n_held], moved[i % n_held]
        left = [bit for bit in (1 << b for b in range(n_blocks.bit_length())) if bit < n_blocks]
        left = [bit for bit in left if bit not in order[:step]]
        here = left.index(order[step])
        mine = (k // order[step]) % 2
        for n in range(keep.shape[0]):
            low = n % (1 << here)
            base = ((n >> here) << (here + 1)) + low
            stay = base + (mine << here)
            leave = base + ((1 - mine) << here)
            keep[n] = source[stay, :, cols] + came[stay, :, cols].astype(F32)
            send[n] = (source[leave, :, cols] + came[leave, :, cols].astype(F32)).astype(BF)


def last_grads_kernel(held_a, held_b, moved_a, moved_b, qkv, proj):
    share = proj.shape[0]
    a = held_a[0] + moved_a[0].astype(F32)
    b = held_b[0] + moved_b[0].astype(F32)
    qkv[0] = a[:, :share].astype(BF)
    qkv[1] = a[:, share:].astype(BF)
    qkv[2] = b[:, :share].astype(BF)
    proj[...] = b[:, share:].T.astype(BF)


def finish_kernel(who, x_in, c_in, gain_in, keep, recv, stats, *refs):
    tokens = keep.shape[1]
    full = x_in.shape[-1]
    own, swap = refs[:2] if len(refs) == 2 else refs[3:5]
    x = x_in[...].reshape(tokens, full)
    standard, inverse = standardize(x)
    sent = recv[2 * tokens :].astype(F32)
    plain = stats[:1] + sent[0:1, :tokens] + sent[1:2, :tokens]
    cross = stats[1:2] + sent[2:3, :tokens] + sent[3:4, :tokens]
    both = stacked_rows((plain, cross), 8, tokens).T
    mean_plain, mean_cross = both[:, 0:1], both[:, 1:2]
    out = halves(x.astype(F32), who)[0] + keep[0] + recv[:tokens].astype(F32)
    scaled = keep[1] + recv[tokens : 2 * tokens].astype(F32)
    scaled = scaled * halves(gain_in[...].reshape(1, full), who)[0]
    through = inverse * (scaled - mean_plain - halves(standard, who)[0] * mean_cross)
    back = halves(c_in[...].reshape(tokens, full).astype(F32), who)[0] + through
    for i, value in enumerate((out, back)):
        a, b = own_and_other(value, who)
        own[i] = a.astype(BF)
        swap[i * tokens : (i + 1) * tokens] = b.astype(BF)
    if len(refs) > 2:
        gains_a, gains_b, recv_other = refs[:3]
        own_gain = refs[5]
        more = recv_other[2 * tokens :].astype(F32)
        total = gains_a[...] + gains_b[...] + sent[4:5] + sent[5:6] + more[4:5] + more[5:6]
        a, b = own_and_other(total, who)
        own_gain[...] = a
        swap[2 * tokens :] = stacked_rows(two_parts(b), 16, b.shape[1]).astype(BF)


def turn(who, held, own, recv, chunk, frame):
    tokens, share = own.shape[1:]
    parity = who[0] % 2
    start = pl.multiple_of(frame * chunk, chunk)
    for i in range(2):
        held[2 * i + parity] = own[i, pl.ds(start, chunk)].astype(F32)
        held[2 * i + 1 - parity] = recv[pl.ds(i * tokens + start, chunk)].astype(F32)
    return held[...].reshape(4 * chunk, share).T.astype(BF)


def pack_early_kernel(frames, slots, who, where, own, recv, *refs):
    outs, held = refs[: len(slots)], refs[len(slots)]
    chunk = own.shape[1] // frames
    for n, s in enumerate(slots):
        outs[n][...] = turn(who, held.at[n], own, recv, chunk, where[0] ^ s)


def pack_late_kernel(frames, slots, who, where, own_a, recv_a, own_b, recv_b, own_gain, *refs):
    outs, held = refs[:frames], refs[frames]
    tokens, share = own_a.shape[1:]
    chunk = tokens // frames
    lanes = outs[0].shape[1]
    sent = recv_a[2 * tokens :].astype(F32)
    value = own_gain[...] + sent[0:1] + sent[1:2]
    n_parts = -(-share // lanes)
    rows = []
    for part in two_parts(value):
        if n_parts * lanes > share:
            part = jnp.concatenate([part, jnp.zeros((1, n_parts * lanes - share), F32)], axis=1)
        rows += [part[:, i * lanes : (i + 1) * lanes] for i in range(n_parts)]
    at = outs[0].shape[0] - 2 * share
    block = stacked_rows(rows, at, lanes).astype(BF)
    for s in range(frames):
        frame = where[0] ^ s
        base = 0
        if s not in slots:
            outs[s][:share] = turn(who, held.at[s, 0], own_b, recv_b, chunk, frame)
            base = share
        outs[s][base : base + share] = turn(who, held.at[s, 1], own_a, recv_a, chunk, frame)
        outs[s][base + share :] = block


def assemble_kernel(n_slots, slots, who, where, *refs):
    soon, parts = refs[: len(slots)], refs[len(slots) : len(slots) + n_slots]
    first, second, total, held, sems = refs[len(slots) + n_slots :]
    lanes = parts[0].shape[1]
    share = first.shape[0]
    middle = lanes // 2
    low_is_late = who[0] // 2 == 0
    copies = []
    value = 0.0
    for s, part in enumerate(parts):
        if s in slots:
            other, base = soon[slots.index(s)][...], 0
        else:
            other, base = part[:share], share
        late = part[base : base + share]
        value = value + part[base + share :].astype(F32)
        low = jnp.where(low_is_late, late, other)
        high = jnp.where(low_is_late, other, late)
        held[s, 0] = jnp.concatenate([low[:, :middle], high[:, :middle]], axis=1)
        held[s, 1] = jnp.concatenate([low[:, middle:], high[:, middle:]], axis=1)
        at = pl.ds(pl.multiple_of((where[0] ^ s) * lanes, lanes), lanes)
        for i, out in enumerate((first, second)):
            copy = pltpu.make_async_copy(held.at[s, i], out.at[:, at], sems.at[2 * s + i])
            copy.start()
            copies.append(copy)
    n_parts = -(-share // lanes)
    value = value[:n_parts] + value[n_parts : 2 * n_parts]
    value = jnp.concatenate([value[i : i + 1] for i in range(n_parts)], axis=1)
    total[...] = value[:, :share]
    for copy in copies:
        copy.wait()


def call(kernel, outs, *args, scalars=1, scratch=(), in_hbm=(), out_hbm=(), limit=None):
    def space(i, hbm):
        return pl.BlockSpec(memory_space=pl.ANY if i in hbm else pltpu.VMEM)

    return pl.pallas_call(
        kernel,
        out_shape=[jax.ShapeDtypeStruct(shape, kind) for shape, kind in outs],
        in_specs=[pl.BlockSpec(memory_space=pltpu.SMEM)] * scalars
        + [space(i, in_hbm) for i in range(scalars, len(args))],
        out_specs=[space(i, out_hbm) for i in range(len(outs))],
        scratch_shapes=scratch,
        compiler_params=pltpu.CompilerParams(vmem_limit_bytes=limit or VMEM_LIMIT),
    )(*args)


EARLY = (7, 6, 5)


def block(frames_in, norm_gain, w_qkv, w_out, keep_runs, out_cotangent):
    _, place_total, width = frames_in.shape
    n_tm, n_te = lax.axis_size("tm"), lax.axis_size("tensor")
    frames = n_tm
    direct = n_tm <= 8
    n_near = n_tm // 2
    chunk = place_total // (n_tm * n_te)
    tokens = frames * chunk
    rows = 16 if chunk % 16 == 0 else chunk
    k = lax.axis_index("tm").astype(jnp.int32)
    j = lax.axis_index("tensor").astype(jnp.int32)
    where, who = k.reshape(1), j.reshape(1)
    share = w_qkv.shape[2]
    pair = 2 * share
    half = width // 2
    lanes = n_te * chunk

    gain = norm_gain

    def gather_chunks(value):
        mine = lax.dynamic_index_in_dim(
            value.reshape(n_tm, n_te, chunk, width), j, 1, keepdims=False
        )
        first = lax.all_to_all(mine, "tm", split_axis=0, concat_axis=0, tiled=True)
        return first, exchange(first, "tensor", 2)

    w_own = jnp.transpose(w_qkv, (1, 2, 0))
    w_other = exchange(w_own, "tensor", 1)
    out_other = exchange(w_out, "tensor", 1)
    if direct:
        (x_mine,) = call(
            send_x_kernel, [((n_tm, chunk, width), BF)],
            who, frames_in.reshape(n_tm, n_te, chunk, width),
            in_hbm=(1,), limit=WHOLE_VMEM,
            scratch=[pltpu.SemaphoreType.DMA((n_tm,))],
        )
        parts = call(
            functools.partial(send_c_kernel, n_near, n_tm),
            [((2, chunk, width), BF)] * n_near + [((chunk, width), BF)] * (n_tm - n_near),
            where, who, out_cotangent.reshape(n_tm, n_te, chunk, width),
            scalars=2, in_hbm=(2,), limit=WHOLE_VMEM,
            scratch=[pltpu.SemaphoreType.DMA((n_tm + n_near,))],
        )
        first = lax.all_to_all(x_mine, "tm", split_axis=0, concat_axis=0, tiled=True)
        xs = (first, exchange(first, "tensor", 2))
        far = [exchange(parts[s], "tm", s) for s in range(n_near, n_tm)]
        (local,) = call(local_kernel, [((2, chunk, width), BF)], parts[0], scalars=0)
        near = [local] + [exchange(parts[s], "tm", s) for s in range(1, n_near)]
        (stacked,) = call(
            stack_kernel, [((n_tm - n_near, chunk, width), BF)], *far,
            scalars=0,
        )
        passed = exchange(stacked, "tensor", 2)
        cs = (near + far, near + [passed] * (n_tm - n_near))
        picks = [
            [0] * n_near + [None] * (n_tm - n_near), [1] * n_near + list(range(n_tm - n_near))
        ]
    else:
        xs = gather_chunks(frames_in)
        cs = tuple([value] for value in gather_chunks(out_cotangent))
        picks = [[None], [None]]
    matrices = (w_own, w_other, w_out, out_other)

    runs = jnp.transpose(keep_runs, (0, 2, 1))
    cube = (frames, chunk)
    done, recvs = [], []
    for g in range(2):
        done.append(
            call(
                functools.partial(attend_kernel, frames, rows, picks[g], n_te, g),
                [
                    (cube + (width,), BF),
                    ((tokens, width), BF),
                    (cube + (pair,), BF),
                    (cube + (3 * pair,), BF),
                    ((2, tokens, half), F32),
                    ((2 * tokens + 16, half), BF),
                    ((2, tokens), F32),
                    ((1, half), F32),
                ],
                who, where, gain, *matrices, runs, xs[g], *cs[g],
                scalars=2,
            )
        )
        recvs.append(exchange(done[g][5], "tensor", 2))

    flat = lambda value: value.reshape(tokens, value.shape[-1])
    grad_parts = [
        call(
            functools.partial(grads_kernel, own),
            [((width, 4 * share), F32 if own else BF)],
            done[0][1], done[1][1], flat(done[0][3]), flat(done[1][3]),
            flat(done[0][0]), flat(done[1][0]), flat(done[0][2]), flat(done[1][2]),
            scalars=0,
        )[0]
        for own in (False, True)
    ]
    grad_send, grad_keep = grad_parts
    grad_recv = exchange(grad_send, "tensor", 1)
    per = width // n_tm
    bits = [1 << i for i in range(n_tm.bit_length() - 1)]
    column = 2 * share
    orders = (bits, bits[1::-1] + bits[2:])
    held = [grad_keep.reshape(n_tm, per, 4 * share)]
    moved = [grad_recv.reshape(n_tm, per, 4 * share)]
    for step in range(len(bits)):
        count = n_tm >> (step + 1)
        piece = (count, per, column)
        result = call(
            functools.partial(halve_kernel, n_tm, orders, step, len(held)),
            [(piece, F32), (piece, BF)] * 2,
            where, *held, *moved,
        )
        held = [result[0], result[2]]
        moved = [exchange(result[2 * i + 1], "tm", orders[i][step]) for i in range(2)]
    grad_qkv, grad_proj = call(
        last_grads_kernel,
        [((3, per, share), BF), ((share, per), BF)],
        *held, *moved,
        scalars=0,
    )
    grad_qkv = jnp.transpose(grad_qkv, (1, 0, 2))

    owns, swapped = [None, None], [None, None]
    for g in (1, 0):
        c_all, _, _, _, keep, _, stats, gains = done[g]
        outs = [((2, tokens, share), BF), ((2 * tokens + (0 if g else 16), share), BF)]
        more = ()
        if g == 0:
            outs.append(((1, share), F32))
            more = (gains, done[1][7], recvs[0])
        result = call(
            finish_kernel, outs,
            who, xs[g], c_all, gain, keep, recvs[1 - g], stats, *more,
        )
        owns[g], swap = result[:2]
        swapped[g] = exchange(swap, "tensor", 1)
        if g == 0:
            own_gain = result[2]

    if direct:
        n_parts = -(-share // lanes)
        extra = -(-2 * n_parts // 16) * 16
        slots = EARLY if n_tm > max(EARLY) else ()
        soon = call(
            functools.partial(pack_early_kernel, frames, slots),
            [((share, lanes), BF)] * len(slots),
            who, where, owns[1], swapped[1], scalars=2,
            scratch=[pltpu.VMEM((len(slots), n_te, chunk, share), F32)],
        ) if slots else []
        soon = [exchange(part, "tm", s) for part, s in zip(soon, slots)]
        messages = call(
            functools.partial(pack_late_kernel, frames, slots),
            [(((1 if s in slots else 2) * share + extra, lanes), BF) for s in range(frames)],
            who, where, owns[0], swapped[0], owns[1], swapped[1], own_gain,
            scalars=2,
            scratch=[pltpu.VMEM((frames, 2, n_te, chunk, share), F32)],
        )
        messages = [messages[0]] + [exchange(messages[s], "tm", s) for s in range(1, n_tm)]
        whole = ((share, place_total), BF)
        block_out, grad_in, total = call(
            functools.partial(assemble_kernel, n_tm, slots),
            [whole, whole, ((1, share), F32)], who, where, *soon, *messages,
            scalars=2, out_hbm=(0, 1),
            scratch=[
                pltpu.VMEM((n_tm, 2, share, lanes), BF), pltpu.SemaphoreType.DMA((2 * n_tm,))
            ],
        )
        block_out, grad_in = block_out.T, grad_in.T
        grad_gain = total.reshape(share)
    else:
        order = jnp.arange(n_te, dtype=jnp.int32) ^ j
        four = jnp.stack(
            [owns[0], swapped[0][: 2 * tokens].reshape(2, tokens, share),
             owns[1], swapped[1].reshape(2, tokens, share)]
        )[order].reshape(n_te, 2, frames, chunk, share)
        message = jnp.transpose(four, (2, 1, 0, 3, 4)).reshape(frames, 2, lanes, share)
        message = lax.all_to_all(message, "tm", split_axis=0, concat_axis=0, tiled=True)
        block_out = message[:, 0].reshape(place_total, share)
        grad_in = message[:, 1].reshape(place_total, share)
        sent = swapped[0][2 * tokens : 2 * tokens + 2].astype(F32)
        grad_gain = lax.psum(own_gain[0] + sent[0] + sent[1], "tm")
    return (block_out[None], grad_in[None], grad_qkv, grad_proj, grad_gain)


def solution(mesh):
    in_specs = (
        P("tm", None, None),
        P(),
        P(None, None, "tensor"),
        P("tensor", None),
        P(),
        P("tm", None, None),
    )
    out_specs = (
        P("tm", None, "tensor"),
        P("tm", None, "tensor"),
        P("tm", None, "tensor"),
        P("tensor", "tm"),
        P("tensor"),
    )
    return jax.shard_map(block, mesh=mesh, in_specs=in_specs, out_specs=out_specs, check_vma=False)
```

```python
import functools

import jax
import jax.numpy as jnp
from jax import lax
from jax.experimental import pallas as pl
from jax.experimental.pallas import tpu as pltpu
from jax.sharding import PartitionSpec as P

D = 768
H = 12
HEAD = D // H
LANES = 128
EPS = 1e-05
MASKED = -1000000000.0

BF = jnp.bfloat16
F32 = jnp.float32
VMEM_LIMIT = 12 * 1024 * 1024
WHOLE_VMEM = 61*1024*1024


def exchange(value, axis, bit):
    size = lax.axis_size(axis)
    return lax.ppermute(value, axis, [(i, i ^ bit) for i in range(size)])


def dot(a, b):
    return lax.dot_general(a, b, (((1,), (0,)), ((), ())), preferred_element_type=F32)


def dot_t(a, b):
    return lax.dot_general(a, b, (((1,), (1,)), ((), ())), preferred_element_type=F32)


def t_dot(a, b):
    return lax.dot_general(a, b, (((0,), (0,)), ((), ())), preferred_element_type=F32)


def standardize(x):
    x = x.astype(F32)
    shifted = x - jnp.mean(x, axis=-1, keepdims=True)
    inverse = lax.rsqrt(jnp.mean(shifted * shifted, axis=-1, keepdims=True) + EPS)
    return shifted * inverse, inverse


def block_rows(value, frames, b, rows):
    q = value.shape[0] // frames
    if q == rows:
        return value
    cut = value.reshape(frames, q, value.shape[1])[:, b * rows : (b + 1) * rows]
    return cut.reshape(frames * rows, value.shape[1])


def split_heads(value):
    lane = lax.broadcasted_iota(jnp.int32, value.shape, 1)
    zero = jnp.zeros_like(value)
    return jnp.concatenate(
        [jnp.where(lane < HEAD, value, zero), jnp.where(lane >= HEAD, value, zero)], axis=0
    )


def join_heads(value):
    n = value.shape[0] // 2
    lane = lax.broadcasted_iota(jnp.int32, (n, value.shape[1]), 1)
    return jnp.where(lane < HEAD, value[:n], value[n:])


def put_rows(ref, b, rows, col, value):
    ref[:, b * rows : (b + 1) * rows, col : col + value.shape[1]] = value.reshape(
        ref.shape[0], rows, value.shape[1]
    )


def all_rows(parts):
    return jnp.concatenate(list(parts), axis=0)


def halves(value, who):
    half = value.shape[-1] // 2
    low, high = value[..., :half], value[..., half:]
    first = who[0] // 2 == 0
    return jnp.where(first, low, high), jnp.where(first, high, low)


def own_and_other(value, who):
    share = value.shape[-1] // 2
    low, high = value[..., :share], value[..., share:]
    first = who[0] % 2 == 0
    return jnp.where(first, low, high), jnp.where(first, high, low)


def two_parts(value):
    top = value.astype(BF).astype(F32)
    return top, value - top


def copy_all(pairs, sems):
    copies = [pltpu.make_async_copy(src, dst, sems.at[i]) for i, (src, dst) in enumerate(pairs)]
    for copy in copies:
        copy.start()
    for copy in copies:
        copy.wait()


def send_x_kernel(j, x_in, x_out, sems):
    copy_all([(x_in.at[i, j[0]], x_out.at[i]) for i in range(x_out.shape[0])], sems)


def send_c_kernel(n_near, n_slots, k, j, c_in, *refs):
    outs, sems = refs[:n_slots], refs[n_slots]
    pairs = []
    for s in range(n_slots):
        if s < n_near:
            for g in range(2):
                pairs.append((c_in.at[k[0] ^ s, j[0] ^ (2 * g)], outs[s].at[g]))
        else:
            pairs.append((c_in.at[k[0] ^ s, j[0]], outs[s]))
    copy_all(pairs, sems)


def stack_kernel(*refs):
    parts, out = refs[:-1], refs[-1]
    for i, ref in enumerate(parts):
        out[i] = ref[...]


def kept_row(runs, frames, rows, first):
    lane = lax.broadcasted_iota(jnp.int32, (frames, frames * rows), 1)
    frame = lax.broadcasted_iota(jnp.int32, (frames, frames * rows), 0)
    place = first + lane % rows
    begins, lengths = runs[:, 0, :], runs[:, 1, :]
    hits = jnp.zeros((frames, frames * rows), F32)
    for r in range(begins.shape[1]):
        begin = begins[:, r : r + 1]
        here = (place >= begin) & (place < begin + lengths[:, r : r + 1])
        hits = jnp.where(here, 1.0, hits)
    return jnp.sum(jnp.where(frame == lane // rows, hits, 0.0), axis=0, keepdims=True)


def attend_kernel(
    frames, rows, picks, n_te, g, who, where, gain_in, wa, wb, oa, ob, runs, x_in, *refs
):
    c_in, rest = refs[: len(picks)], refs[len(picks) :]
    c_all, normed, mixed, pcot, keep, send, stats, gains = rest
    if len(picks) == 1:
        c_all[...] = c_in[0][...]
    else:
        for s, (ref, pick) in enumerate(zip(c_in, picks)):
            c_all[where[0] ^ s] = ref[...] if pick is None else ref[pick]
    gain = gain_in[...].reshape(1, x_in.shape[2])
    wq, wk, wv = (all_rows((wa[i], wb[i])) for i in range(3))
    wout = all_rows((oa[...], ob[...]))
    width, full = wout.shape
    chunk = x_in.shape[1]
    tokens = frames * chunk
    n_rows = frames * rows
    standard, _ = standardize(x_in[...].reshape(tokens, full))
    n = (standard * gain).astype(BF)
    normed[...] = n
    qs, ks, vs = (dot_t(n, w).astype(BF) for w in (wq, wk, wv))
    c = c_all[...].reshape(tokens, full)
    mc = dot_t(c, wout).astype(BF)
    row = lax.broadcasted_iota(jnp.int32, (n_rows, n_rows), 0)
    col = lax.broadcasted_iota(jnp.int32, (n_rows, n_rows), 1)
    first = (where[0] * n_te + (who[0] ^ (2 * g))) * chunk
    for b in range(chunk // rows):
        across = kept_row(runs, frames, rows, first + b * rows)
        down = jnp.sum(jnp.where(row == col, across, 0.0), axis=1, keepdims=True)
        inside = jnp.where(row % rows == col % rows, across * down, 0.0)
        for p in range(width // LANES):
            cols = slice(p * LANES, (p + 1) * LANES)
            q, k, v, dm = (block_rows(z[:, cols], frames, b, rows) for z in (qs, ks, vs, mc))
            kk, vv = split_heads(k), split_heads(v)
            s = dot_t(q, kk) * HEAD ** (-0.5)
            dw = dot_t(dm, vv).astype(BF).astype(F32)
            w_parts, d_parts = [], []
            for e in range(2):
                part = jnp.where(inside > 0, s[:, e * n_rows : (e + 1) * n_rows], MASKED)
                top = jnp.max(part, axis=-1, keepdims=True)
                ex = jnp.exp(part - top) * inside
                total = jnp.sum(ex, axis=-1, keepdims=True)
                we = ex / jnp.where(total > 0, total, 1.0)
                de = dw[:, e * n_rows : (e + 1) * n_rows]
                inner = jnp.sum(we * de, axis=-1, keepdims=True)
                w_parts.append(we.astype(BF))
                d_parts.append((we * (de - inner) * HEAD ** (-0.5)).astype(BF))
            w = jnp.concatenate(w_parts, axis=1)
            ds = jnp.concatenate(d_parts, axis=1)
            put_rows(mixed, b, rows, p * LANES, dot(w, vv).astype(BF))
            put_rows(pcot, b, rows, p * LANES, dot(ds, kk).astype(BF))
            put_rows(pcot, b, rows, width + p * LANES, join_heads(t_dot(ds, q)).astype(BF))
            put_rows(pcot, b, rows, 2 * width + p * LANES, join_heads(t_dot(w, dm)).astype(BF))
    y = dot(mixed[...].reshape(tokens, width), wout)
    mine, other = halves(y, who)
    keep[0] = mine
    send[:tokens] = other.astype(BF)
    pc = pcot[...].reshape(tokens, 3 * width)
    nc = dot(pc, all_rows((wq, wk, wv)))
    nn = n.astype(F32) * nc
    mean_plain = jnp.sum(nc * gain, axis=-1, keepdims=True)
    mean_cross = jnp.sum(nn, axis=-1, keepdims=True)
    total_gain = jnp.sum(nn, axis=0, keepdims=True) / gain
    lane = lax.broadcasted_iota(jnp.int32, (tokens, LANES), 1)
    both = (jnp.where(lane == 0, mean_plain, mean_cross) * (1.0 / full)).T[:2]
    half = full // 2
    stats[...] = both
    mine, other = halves(nc, who)
    keep[1] = mine
    send[tokens : 2 * tokens] = other.astype(BF)
    mine, other = halves(total_gain, who)
    gains[...] = mine
    if half > tokens:
        both = jnp.concatenate([both, jnp.zeros((2, half - tokens), F32)], axis=1)
    sent = []
    for value in (both[:1], both[1:], other):
        sent += two_parts(value)
    send[2 * tokens :] = stacked_rows(sent, 16, half).astype(BF)


def stacked_rows(values, count, lanes):
    at = lax.broadcasted_iota(jnp.int32, (count, lanes), 0)
    block = jnp.zeros((count, lanes), F32)
    for i, value in enumerate(values):
        block = jnp.where(at == i, value, block)
    return block


def local_kernel(source, out):
    out[...] = source[...]


def grads_kernel(own, n0, n1, p0, p1, c0, c1, m0, m1, out):
    width = m0.shape[1]
    share = width // 2
    columns = []
    for which in range(4):
        if which < 3:
            left, right, base = (n0, n1), (p0, p1), which * width
        else:
            left, right, base = (c0, c1), (m0, m1), 0
        cols = slice(base, base + width)
        value = t_dot(left[0][...], right[0][:, cols]) + t_dot(left[1][...], right[1][:, cols])
        columns.append(value[:, :share] if own else value[:, share:])
    out[...] = jnp.concatenate(columns, axis=1).astype(out.dtype)


def halve_kernel(n_blocks, orders, step, n_held, where, *refs):
    held, moved, outs = refs[:n_held], refs[n_held : 2 * n_held], refs[2 * n_held :]
    k = where[0]
    for i, order in enumerate(orders):
        column = outs[2 * i].shape[-1]
        cols = slice(i * column, (i + 1) * column) if n_held == 1 else slice(None)
        keep, send = outs[2 * i : 2 * i + 2]
        source, came = held[i % n_held], moved[i % n_held]
        left = [bit for bit in (1 << b for b in range(n_blocks.bit_length())) if bit < n_blocks]
        left = [bit for bit in left if bit not in order[:step]]
        here = left.index(order[step])
        mine = (k // order[step]) % 2
        for n in range(keep.shape[0]):
            low = n % (1 << here)
            base = ((n >> here) << (here + 1)) + low
            stay = base + (mine << here)
            leave = base + ((1 - mine) << here)
            keep[n] = source[stay, :, cols] + came[stay, :, cols].astype(F32)
            send[n] = (source[leave, :, cols] + came[leave, :, cols].astype(F32)).astype(BF)


def last_grads_kernel(held_a, held_b, moved_a, moved_b, qkv, proj):
    share = proj.shape[0]
    a = held_a[0] + moved_a[0].astype(F32)
    b = held_b[0] + moved_b[0].astype(F32)
    qkv[0] = a[:, :share].astype(BF)
    qkv[1] = a[:, share:].astype(BF)
    qkv[2] = b[:, :share].astype(BF)
    proj[...] = b[:, share:].T.astype(BF)


def finish_kernel(who, x_in, c_in, gain_in, keep, recv, stats, *refs):
    tokens = keep.shape[1]
    full = x_in.shape[-1]
    own, swap = refs[:2] if len(refs) == 2 else refs[3:5]
    x = x_in[...].reshape(tokens, full)
    standard, inverse = standardize(x)
    sent = recv[2 * tokens :].astype(F32)
    plain = stats[:1] + sent[0:1, :tokens] + sent[1:2, :tokens]
    cross = stats[1:2] + sent[2:3, :tokens] + sent[3:4, :tokens]
    both = stacked_rows((plain, cross), 8, tokens).T
    mean_plain, mean_cross = both[:, 0:1], both[:, 1:2]
    out = halves(x.astype(F32), who)[0] + keep[0] + recv[:tokens].astype(F32)
    scaled = keep[1] + recv[tokens : 2 * tokens].astype(F32)
    scaled = scaled * halves(gain_in[...].reshape(1, full), who)[0]
    through = inverse * (scaled - mean_plain - halves(standard, who)[0] * mean_cross)
    back = halves(c_in[...].reshape(tokens, full).astype(F32), who)[0] + through
    for i, value in enumerate((out, back)):
        a, b = own_and_other(value, who)
        own[i] = a.astype(BF)
        swap[i * tokens : (i + 1) * tokens] = b.astype(BF)
    if len(refs) > 2:
        gains_a, gains_b, recv_other = refs[:3]
        own_gain = refs[5]
        more = recv_other[2 * tokens :].astype(F32)
        total = gains_a[...] + gains_b[...] + sent[4:5] + sent[5:6] + more[4:5] + more[5:6]
        a, b = own_and_other(total, who)
        own_gain[...] = a
        swap[2 * tokens :] = stacked_rows(two_parts(b), 16, b.shape[1]).astype(BF)


def turn(who, held, own, recv, chunk, frame):
    tokens, share = own.shape[1:]
    parity = who[0] % 2
    start = pl.multiple_of(frame * chunk, chunk)
    for i in range(2):
        held[2 * i + parity] = own[i, pl.ds(start, chunk)].astype(F32)
        held[2 * i + 1 - parity] = recv[pl.ds(i * tokens + start, chunk)].astype(F32)
    return held[...].reshape(4 * chunk, share).T.astype(BF)


def pack_early_kernel(frames, slots, who, where, own, recv, *refs):
    outs, held = refs[: len(slots)], refs[len(slots)]
    chunk = own.shape[1] // frames
    for n, s in enumerate(slots):
        outs[n][...] = turn(who, held.at[n], own, recv, chunk, where[0] ^ s)


def pack_late_kernel(frames, slots, who, where, own_a, recv_a, own_b, recv_b, own_gain, *refs):
    outs, held = refs[:frames], refs[frames]
    tokens, share = own_a.shape[1:]
    chunk = tokens // frames
    lanes = outs[0].shape[1]
    sent = recv_a[2 * tokens :].astype(F32)
    value = own_gain[...] + sent[0:1] + sent[1:2]
    n_parts = -(-share // lanes)
    rows = []
    for part in two_parts(value):
        if n_parts * lanes > share:
            part = jnp.concatenate([part, jnp.zeros((1, n_parts * lanes - share), F32)], axis=1)
        rows += [part[:, i * lanes : (i + 1) * lanes] for i in range(n_parts)]
    at = outs[0].shape[0] - 2 * share
    block = stacked_rows(rows, at, lanes).astype(BF)
    for s in range(frames):
        frame = where[0] ^ s
        base = 0
        if s not in slots:
            outs[s][:share] = turn(who, held.at[s, 0], own_b, recv_b, chunk, frame)
            base = share
        outs[s][base : base + share] = turn(who, held.at[s, 1], own_a, recv_a, chunk, frame)
        outs[s][base + share :] = block


def assemble_kernel(picks, slots, continuing, who, where, *refs):
    soon_slots = [s for s in picks if s in slots]
    soon, refs = refs[: len(soon_slots)], refs[len(soon_slots) :]
    parts, refs = refs[: len(picks)], refs[len(picks) :]
    before, refs = refs[: 3 * continuing], refs[3 * continuing :]
    first, second, total, held, sems = refs
    lanes = parts[0].shape[1]
    share = first.shape[0]
    middle = lanes // 2
    low_is_late = who[0] // 2 == 0
    copies = []
    value = 0.0
    for n, (s, part) in enumerate(zip(picks, parts)):
        if s in slots:
            other, base = soon[soon_slots.index(s)][...], 0
        else:
            other, base = part[:share], share
        late = part[base : base + share]
        value = value + part[base + share :].astype(F32)
        low = jnp.where(low_is_late, late, other)
        high = jnp.where(low_is_late, other, late)
        held[n, 0] = jnp.concatenate([low[:, :middle], high[:, :middle]], axis=1)
        held[n, 1] = jnp.concatenate([low[:, middle:], high[:, middle:]], axis=1)
        at = pl.ds(pl.multiple_of((where[0] ^ s) * lanes, lanes), lanes)
        for i, out in enumerate((first, second)):
            copy = pltpu.make_async_copy(held.at[n, i], out.at[:, at], sems.at[2 * n + i])
            copy.start()
            copies.append(copy)
    n_parts = -(-share // lanes)
    value = value[:n_parts] + value[n_parts : 2 * n_parts]
    value = jnp.concatenate([value[i : i + 1] for i in range(n_parts)], axis=1)[:, :share]
    total[...] = value + before[2][...] if continuing else value
    for copy in copies:
        copy.wait()


def call(
    kernel, outs, *args, scalars=1, scratch=(), in_hbm=(), out_hbm=(), limit=None,
    aliases=None,
):
    def space(i, hbm):
        return pl.BlockSpec(memory_space=pl.ANY if i in hbm else pltpu.VMEM)

    return pl.pallas_call(
        kernel,
        out_shape=[jax.ShapeDtypeStruct(shape, kind) for shape, kind in outs],
        in_specs=[pl.BlockSpec(memory_space=pltpu.SMEM)] * scalars
        + [space(i, in_hbm) for i in range(scalars, len(args))],
        out_specs=[space(i, out_hbm) for i in range(len(outs))],
        scratch_shapes=scratch,
        input_output_aliases=aliases or {},
        compiler_params=pltpu.CompilerParams(vmem_limit_bytes=limit or VMEM_LIMIT),
    )(*args)


EARLY = (7, 6, 5)
LAST = (4, 3, 2, 1)


def block(frames_in, norm_gain, w_qkv, w_out, keep_runs, out_cotangent):
    _, place_total, width = frames_in.shape
    n_tm, n_te = lax.axis_size("tm"), lax.axis_size("tensor")
    frames = n_tm
    direct = n_tm <= 8
    n_near = n_tm // 2
    chunk = place_total // (n_tm * n_te)
    tokens = frames * chunk
    rows = 16 if chunk % 16 == 0 else chunk
    k = lax.axis_index("tm").astype(jnp.int32)
    j = lax.axis_index("tensor").astype(jnp.int32)
    where, who = k.reshape(1), j.reshape(1)
    share = w_qkv.shape[2]
    pair = 2 * share
    half = width // 2
    lanes = n_te * chunk

    gain = norm_gain

    def gather_chunks(value):
        mine = lax.dynamic_index_in_dim(
            value.reshape(n_tm, n_te, chunk, width), j, 1, keepdims=False
        )
        first = lax.all_to_all(mine, "tm", split_axis=0, concat_axis=0, tiled=True)
        return first, exchange(first, "tensor", 2)

    w_own = jnp.transpose(w_qkv, (1, 2, 0))
    w_other = exchange(w_own, "tensor", 1)
    out_other = exchange(w_out, "tensor", 1)
    if direct:
        (x_mine,) = call(
            send_x_kernel, [((n_tm, chunk, width), BF)],
            who, frames_in.reshape(n_tm, n_te, chunk, width),
            in_hbm=(1,), limit=WHOLE_VMEM,
            scratch=[pltpu.SemaphoreType.DMA((n_tm,))],
        )
        parts = call(
            functools.partial(send_c_kernel, n_near, n_tm),
            [((2, chunk, width), BF)] * n_near + [((chunk, width), BF)] * (n_tm - n_near),
            where, who, out_cotangent.reshape(n_tm, n_te, chunk, width),
            scalars=2, in_hbm=(2,), limit=WHOLE_VMEM,
            scratch=[pltpu.SemaphoreType.DMA((n_tm + n_near,))],
        )
        first = lax.all_to_all(x_mine, "tm", split_axis=0, concat_axis=0, tiled=True)
        xs = (first, exchange(first, "tensor", 2))
        far = [exchange(parts[s], "tm", s) for s in range(n_near, n_tm)]
        (local,) = call(local_kernel, [((2, chunk, width), BF)], parts[0], scalars=0)
        near = [local] + [exchange(parts[s], "tm", s) for s in range(1, n_near)]
        (stacked,) = call(
            stack_kernel, [((n_tm - n_near, chunk, width), BF)], *far,
            scalars=0,
        )
        passed = exchange(stacked, "tensor", 2)
        cs = (near + far, near + [passed] * (n_tm - n_near))
        picks = [
            [0] * n_near + [None] * (n_tm - n_near), [1] * n_near + list(range(n_tm - n_near))
        ]
    else:
        xs = gather_chunks(frames_in)
        cs = tuple([value] for value in gather_chunks(out_cotangent))
        picks = [[None], [None]]
    matrices = (w_own, w_other, w_out, out_other)

    runs = jnp.transpose(keep_runs, (0, 2, 1))
    cube = (frames, chunk)
    done, recvs = [], []
    for g in range(2):
        done.append(
            call(
                functools.partial(attend_kernel, frames, rows, picks[g], n_te, g),
                [
                    (cube + (width,), BF),
                    ((tokens, width), BF),
                    (cube + (pair,), BF),
                    (cube + (3 * pair,), BF),
                    ((2, tokens, half), F32),
                    ((2 * tokens + 16, half), BF),
                    ((2, tokens), F32),
                    ((1, half), F32),
                ],
                who, where, gain, *matrices, runs, xs[g], *cs[g],
                scalars=2,
            )
        )
        recvs.append(exchange(done[g][5], "tensor", 2))

    flat = lambda value: value.reshape(tokens, value.shape[-1])
    grad_parts = [
        call(
            functools.partial(grads_kernel, own),
            [((width, 4 * share), F32 if own else BF)],
            done[0][1], done[1][1], flat(done[0][3]), flat(done[1][3]),
            flat(done[0][0]), flat(done[1][0]), flat(done[0][2]), flat(done[1][2]),
            scalars=0,
        )[0]
        for own in (False, True)
    ]
    grad_send, grad_keep = grad_parts
    grad_recv = exchange(grad_send, "tensor", 1)
    per = width // n_tm
    bits = [1 << i for i in range(n_tm.bit_length() - 1)]
    column = 2 * share
    orders = (bits, bits[1::-1] + bits[2:])
    held = [grad_keep.reshape(n_tm, per, 4 * share)]
    moved = [grad_recv.reshape(n_tm, per, 4 * share)]
    for step in range(len(bits)):
        count = n_tm >> (step + 1)
        piece = (count, per, column)
        result = call(
            functools.partial(halve_kernel, n_tm, orders, step, len(held)),
            [(piece, F32), (piece, BF)] * 2,
            where, *held, *moved,
        )
        held = [result[0], result[2]]
        moved = [exchange(result[2 * i + 1], "tm", orders[i][step]) for i in range(2)]
    grad_qkv, grad_proj = call(
        last_grads_kernel,
        [((3, per, share), BF), ((share, per), BF)],
        *held, *moved,
        scalars=0,
    )
    grad_qkv = jnp.transpose(grad_qkv, (1, 0, 2))

    owns, swapped = [None, None], [None, None]
    for g in (1, 0):
        c_all, _, _, _, keep, _, stats, gains = done[g]
        outs = [((2, tokens, share), BF), ((2 * tokens + (0 if g else 16), share), BF)]
        more = ()
        if g == 0:
            outs.append(((1, share), F32))
            more = (gains, done[1][7], recvs[0])
        result = call(
            finish_kernel, outs,
            who, xs[g], c_all, gain, keep, recvs[1 - g], stats, *more,
        )
        owns[g], swap = result[:2]
        swapped[g] = exchange(swap, "tensor", 1)
        if g == 0:
            own_gain = result[2]

    if direct:
        n_parts = -(-share // lanes)
        extra = -(-2 * n_parts // 16) * 16
        slots = EARLY if n_tm > max(EARLY) else ()
        soon = call(
            functools.partial(pack_early_kernel, frames, slots),
            [((share, lanes), BF)] * len(slots),
            who, where, owns[1], swapped[1], scalars=2,
            scratch=[pltpu.VMEM((len(slots), n_te, chunk, share), F32)],
        ) if slots else []
        soon = [exchange(part, "tm", s) for part, s in zip(soon, slots)]
        messages = call(
            functools.partial(pack_late_kernel, frames, slots),
            [(((1 if s in slots else 2) * share + extra, lanes), BF) for s in range(frames)],
            who, where, owns[0], swapped[0], owns[1], swapped[1], own_gain,
            scalars=2,
            scratch=[pltpu.VMEM((frames, 2, n_te, chunk, share), F32)],
        )
        messages = [messages[0]] + [exchange(messages[s], "tm", s) for s in range(1, n_tm)]
        whole = ((share, place_total), BF)
        early = dict(zip(slots, soon))
        last = [s for s in (LAST if slots else ()) if s < n_tm]
        placed = []
        for picks in ([s for s in range(n_tm) if s not in last], last):
            if not picks:
                continue
            args = [early[s] for s in picks if s in early] + [messages[s] for s in picks]
            at = 2 + len(args)
            placed = call(
                functools.partial(assemble_kernel, picks, slots, bool(placed)),
                [whole, whole, ((1, share), F32)], who, where, *args, *placed,
                scalars=2, in_hbm=(at, at + 1), out_hbm=(0, 1),
                aliases={at: 0, at + 1: 1} if placed else None,
                scratch=[
                    pltpu.VMEM((len(picks), 2, share, lanes), BF),
                    pltpu.SemaphoreType.DMA((2 * len(picks),)),
                ],
            )
        block_out, grad_in, total = placed
        block_out, grad_in = block_out.T, grad_in.T
        grad_gain = total.reshape(share)
    else:
        order = jnp.arange(n_te, dtype=jnp.int32) ^ j
        four = jnp.stack(
            [owns[0], swapped[0][: 2 * tokens].reshape(2, tokens, share),
             owns[1], swapped[1].reshape(2, tokens, share)]
        )[order].reshape(n_te, 2, frames, chunk, share)
        message = jnp.transpose(four, (2, 1, 0, 3, 4)).reshape(frames, 2, lanes, share)
        message = lax.all_to_all(message, "tm", split_axis=0, concat_axis=0, tiled=True)
        block_out = message[:, 0].reshape(place_total, share)
        grad_in = message[:, 1].reshape(place_total, share)
        sent = swapped[0][2 * tokens : 2 * tokens + 2].astype(F32)
        grad_gain = lax.psum(own_gain[0] + sent[0] + sent[1], "tm")
    return (block_out[None], grad_in[None], grad_qkv, grad_proj, grad_gain)


def solution(mesh):
    in_specs = (
        P("tm", None, None),
        P(),
        P(None, None, "tensor"),
        P("tensor", None),
        P(),
        P("tm", None, None),
    )
    out_specs = (
        P("tm", None, "tensor"),
        P("tm", None, "tensor"),
        P("tm", None, "tensor"),
        P("tensor", "tm"),
        P("tensor"),
    )
    return jax.shard_map(block, mesh=mesh, in_specs=in_specs, out_specs=out_specs, check_vma=False)
```
